768 devices in a mesh: seq: 64 (over y, x, core), head: 12 (over z).
Axes of the slice: x: 4, y: 8, z: 12, core: 2. Of those that a mesh axis runs over, the one named last changes fastest.
Arguments:
- lin_query: bfloat16 [8192, 6144], P('seq', 'head'), may hold values from -0.52734375 to 0.52734375
- lin_key: bfloat16 [8192, 6144], P('seq', 'head'), may hold values from -0.52734375 to 0.52734375
- lin_value: bfloat16 [8192, 6144], P('seq', 'head'), may hold values from -6 to 6
- log_decay: float32 [48, 8192], P('head', 'seq'), may hold values from -1.5 to 0
- out_gate: bfloat16 [8192, 6144], P('seq', 'head'), may hold values from -8 to 8
- norm_gain: float32 [6144], P('head'), may hold values from 0.25 to 1.75
- soft_query: bfloat16 [8192, 6144], P('seq', 'head'), may hold values from -8 to 8
- soft_key: bfloat16 [8192, 768], P('seq'), may hold values from -6 to 6
- soft_value: bfloat16 [8192, 768], P('seq'), may hold values from -6 to 6
- segment_of: int32 [64], replicated, may hold values from 0 to 63, each once
Outputs:
- lin_out: bfloat16 [8192, 6144], P('seq', 'head')
- soft_out: bfloat16 [8192, 6144], P('seq', 'head')
The draws below stay inside these ranges and needn't reach their ends.
Inputs may be any that keep to these rules, and one draw needn't show every extreme that they name: `segment_of`: each segment number stands once.
All inputs are finite; a program needn't handle non-finite values.
Results may differ from the reference program's by a relative error of at most 0.008.
Values may be sent and summed in bfloat16 or wider, within the bound.
No kernel may reach another device: no remote copies, remote signals or barrier semaphores. Data moves between devices by JAX's collectives and lax.ppermute only.
A program may use at most 128 MiB of HBM per device.

```python
import math
import jax
import jax.numpy as jnp
from jax import lax

HEAD_DIM = 128
Q_PER_KV = 8
TOK_DEV = 128
QUERY_HEAD_COUNT = 48
KV_HEADS = 6
TOKEN_COUNT = 8192
SEGMENTS = 64


def draw_log_decay(key, part):
    random_key_root, random_key_noise, random_key_block, random_key_spike, random_key_depth = jax.random.split(key, 5)
    log_low = math.log(0.2 / TOKEN_COUNT)
    log_high = math.log(1.0 / 30.0)
    base_rate = jnp.exp(jax.random.uniform(random_key_root, (QUERY_HEAD_COUNT, 1), jnp.float32, log_low, log_high))
    jitter = jax.random.uniform(random_key_noise, (QUERY_HEAD_COUNT, TOKEN_COUNT), jnp.float32, 0.5, 2.0)
    block_count = TOKEN_COUNT // TOK_DEV
    block_log = jax.random.uniform(random_key_block, (QUERY_HEAD_COUNT, block_count, 1), jnp.float32, math.log(0.5), math.log(2.0))
    block_factor = jnp.broadcast_to(jnp.exp(block_log), (QUERY_HEAD_COUNT, block_count, TOK_DEV)).reshape(QUERY_HEAD_COUNT, TOKEN_COUNT)
    spike_strike = jax.random.uniform(random_key_spike, (QUERY_HEAD_COUNT, TOKEN_COUNT), jnp.float32, 0.0, 1.0) < 3.0 / TOKEN_COUNT
    spike_depth = jax.random.uniform(random_key_depth, (QUERY_HEAD_COUNT, TOKEN_COUNT), jnp.float32, 0.2, 0.7)
    steady_level = -(base_rate * jitter * block_factor)
    return steady_level + jnp.where(spike_strike, jnp.log(1.0 - spike_depth), 0.0)


def draw_soft_query(key, part):
    width = QUERY_HEAD_COUNT * HEAD_DIM
    drawn_key = jax.random.fold_in(key, 11)
    return jnp.clip(jax.random.normal(drawn_key, (TOKEN_COUNT, width), jnp.float32), -6.0, 6.0).astype(jnp.bfloat16)


def draw_soft_key(key, part):
    width = KV_HEADS * HEAD_DIM
    drawn_key = jax.random.fold_in(key, 12)
    return jnp.clip(jax.random.normal(drawn_key, (TOKEN_COUNT, width), jnp.float32), -6.0, 6.0).astype(jnp.bfloat16)


def block_scale(rng, extent, cuts, low, high):
    factor_of = 1.0
    for axis_at, shards_of in cuts:
        steps = jax.random.uniform(jax.random.fold_in(jax.random.fold_in(rng, 6), axis_at), (shards_of,), jnp.float32, low / len(cuts), high / len(cuts))
        factor_of = factor_of * jnp.repeat(jnp.exp(steps), extent[axis_at] // shards_of).reshape((-1,) + (1,) * (len(extent) - 1 - axis_at))
    return factor_of


def scatter_about(key, extent, scale, reach, pieces=(), kind=jnp.bfloat16):
    values = jax.random.normal(key, extent, jnp.float32) * scale
    if len(pieces) > 0:
        values = block_scale(key, extent, pieces, -0.22, 0.18) * values
    return jnp.clip(values, min=-reach, max=reach).astype(kind)


def setup_inputs(seed: int = 0) -> dict:
    splits = jax.random.split(jax.random.key(seed), 11)
    return {
        "lin_query": scatter_about(splits[0], (TOKEN_COUNT, QUERY_HEAD_COUNT * HEAD_DIM), (HEAD_DIM ** -0.5), 0.52734375, ((0, 64), (1, 12))),
        "lin_key": scatter_about(splits[1], (TOKEN_COUNT, QUERY_HEAD_COUNT * HEAD_DIM), (HEAD_DIM ** -0.5), 0.52734375, ((0, 64), (1, 12))),
        "lin_value": scatter_about(splits[2], (TOKEN_COUNT, QUERY_HEAD_COUNT * HEAD_DIM), 1.0, 6.0, ((0, 64), (1, 12))),
        "log_decay": draw_log_decay(jax.random.fold_in(splits[10], 71), 0),
        "out_gate": scatter_about(splits[4], (TOKEN_COUNT, QUERY_HEAD_COUNT * HEAD_DIM), 1.5, 8.0, ((0, 64), (1, 12))),
        "norm_gain": jnp.clip(1.0 + 0.15 * jax.random.normal(splits[5], (QUERY_HEAD_COUNT * HEAD_DIM,), jnp.float32), 0.25, 1.75),
        "soft_query": draw_soft_query(jax.random.fold_in(splits[10], 71), 0),
        "soft_key": draw_soft_key(jax.random.fold_in(splits[10], 71), 0),
        "soft_value": scatter_about(splits[8], (TOKEN_COUNT, KV_HEADS * HEAD_DIM), 1.0, 6.0, ((0, 64),)),
        "segment_of": jax.random.permutation(splits[9], SEGMENTS).astype(jnp.int32),
    }


norm_eps = 1e-06

def rounded(values_in):
    return lax.optimization_barrier(values_in.astype(jnp.bfloat16)).astype(jnp.float32)

def decay_weights(cumulative):
    row_count = cumulative.shape[1]
    positions = jnp.arange(row_count, dtype=jnp.int32)
    causal_mask = positions[:, None] >= positions[None, :]
    spread = cumulative[:, :, None] - cumulative[:, None, :]
    return jnp.where(causal_mask[None], jnp.exp(jnp.where(causal_mask[None], spread, 0.0)), 0.0)

def lightning_layer(lin_query, lin_key, lin_value, log_decay, out_gate, norm_gain):
    blocks = TOKEN_COUNT // TOK_DEV

    def to_blocks(array):
        return array.reshape(blocks, TOK_DEV, QUERY_HEAD_COUNT, HEAD_DIM).astype(jnp.float32)
    decays = log_decay.reshape(QUERY_HEAD_COUNT, blocks, TOK_DEV).transpose(1, 0, 2)

    def advance(memory, inputs):
        query_heads, key_heads, value_heads, block_log = inputs
        cumulative = jnp.cumsum(block_log, axis=1)
        scores = jnp.einsum('thd,shd->hts', query_heads, key_heads)
        mixing = rounded(scores * decay_weights(cumulative))
        inside = jnp.einsum('hts,shd->thd', mixing, value_heads)
        tail_decay = jnp.exp(cumulative[:, -1:] - cumulative)
        weighted_keys = key_heads * tail_decay.T[:, :, None]
        local_memory = jnp.einsum('thd,the->hde', weighted_keys, value_heads, precision=lax.Precision.HIGHEST)
        lifted = query_heads * jnp.exp(cumulative).T[:, :, None]
        earlier_part = jnp.einsum('thd,hde->the', lifted, memory, precision=lax.Precision.HIGHEST)
        new_memory = jnp.exp(cumulative[:, -1])[:, None, None] * memory + local_memory
        return (new_memory, inside + earlier_part)
    start_memory = jnp.zeros((QUERY_HEAD_COUNT, HEAD_DIM, HEAD_DIM), jnp.float32)
    final_memory, mixed_out = lax.scan(advance, start_memory, (to_blocks(lin_query), to_blocks(lin_key), to_blocks(lin_value), decays))
    mixed_out = mixed_out.reshape(TOKEN_COUNT, QUERY_HEAD_COUNT * HEAD_DIM)
    inverse_rms = lax.rsqrt(lax.optimization_barrier(jnp.mean(mixed_out * mixed_out, axis=1)) + norm_eps)
    gated = mixed_out * inverse_rms[:, None] * norm_gain[None, :] * jax.nn.sigmoid(out_gate.astype(jnp.float32))
    return gated.astype(jnp.bfloat16)

def softmax_layer(soft_query, soft_key, soft_value, segment_of):
    row_ids = jnp.arange(TOKEN_COUNT, dtype=jnp.int32)
    positions = segment_of[row_ids // TOK_DEV] * TOK_DEV + row_ids % TOK_DEV
    query_heads = soft_query.reshape(TOKEN_COUNT, KV_HEADS, Q_PER_KV, HEAD_DIM).transpose(1, 0, 2, 3)
    key_heads = soft_key.reshape(TOKEN_COUNT, KV_HEADS, HEAD_DIM).transpose(1, 0, 2)
    value_heads = soft_value.reshape(TOKEN_COUNT, KV_HEADS, HEAD_DIM).transpose(1, 0, 2)
    blocks = TOKEN_COUNT // TOK_DEV
    score_scale = HEAD_DIM ** (-0.5)

    def one_head(inputs):
        head_query, head_key, head_value = inputs
        key_float = head_key.astype(jnp.float32)
        value_float = head_value.astype(jnp.float32)

        def one_block(block_index):
            block_query = lax.dynamic_slice_in_dim(head_query, block_index * TOK_DEV, TOK_DEV, 0)
            block_pos = lax.dynamic_slice_in_dim(positions, block_index * TOK_DEV, TOK_DEV, 0)
            logits = jnp.einsum('tgd,sd->gts', block_query.astype(jnp.float32), key_float) * score_scale
            visible = positions[None, :] <= block_pos[:, None]
            logits = jnp.where(visible[None], logits, -1e+30)
            row_peak = lax.optimization_barrier(jnp.max(logits, axis=2))
            weights_now = jnp.where(visible[None], jnp.exp(logits - row_peak[:, :, None]), 0.0)
            totals = lax.optimization_barrier(jnp.sum(weights_now, axis=2))
            summed = jnp.einsum('gts,sd->gtd', rounded(weights_now), value_float)
            return (summed / totals[:, :, None]).transpose(1, 0, 2)
        return lax.map(one_block, jnp.arange(blocks, dtype=jnp.int32))
    outputs = lax.map(one_head, (query_heads, key_heads, value_heads))
    return outputs.transpose(1, 2, 0, 3, 4).reshape(TOKEN_COUNT, QUERY_HEAD_COUNT * HEAD_DIM).astype(jnp.bfloat16)

def reference(lin_query, lin_key, lin_value, log_decay, out_gate, norm_gain, soft_query, soft_key, soft_value, segment_of):
    lin_out = lightning_layer(lin_query, lin_key, lin_value, log_decay, out_gate, norm_gain)
    soft_out = softmax_layer(soft_query, soft_key, soft_value, segment_of)
    return (lin_out, soft_out)
```

```python
import jax
import jax.numpy as jnp
from jax import lax
from jax.experimental import pallas as pl
from jax.experimental.pallas import tpu as pltpu
from jax.sharding import PartitionSpec as P


HEAD_DIM = 128
HEADS_DEV = 4
Q_PER_KV = 8
TOK = 128
SEGS = 64
HALF = 32
ROWS = 8
COLUMNS = 4
KEY_BLOCK = 8

norm_eps = 1e-06
SCALE = HEAD_DIM ** (-0.5)
LOG2E = 1.4426950408889634
F32 = jnp.float32
BF16 = jnp.bfloat16
MASKED = -1e30

VM = pl.BlockSpec(memory_space=pltpu.VMEM)
SM = pl.BlockSpec(memory_space=pltpu.SMEM)


def dot(a, b, ca, cb, precision=None):
    return lax.dot_general(
        a, b, (((ca,), (cb,)), ((), ())), precision=precision, preferred_element_type=F32
    )


def iotas(n=TOK):
    return (
        lax.broadcasted_iota(jnp.int32, (n, TOK), 0),
        lax.broadcasted_iota(jnp.int32, (n, TOK), 1),
    )


def cumulative_columns(log_row):
    row, col = iotas()
    wide = jnp.broadcast_to(log_row, (TOK, TOK))
    column = jnp.sum(jnp.where(col <= row, wide, 0.0), axis=1, keepdims=True)
    log_column = jnp.sum(jnp.where(col == row, wide, 0.0), axis=1, keepdims=True)
    as_row = jnp.sum(jnp.where(row <= col, log_column, 0.0), axis=0, keepdims=True)
    return column, as_row


def split_bf16(value):
    high = value.astype(BF16)
    return high, (value - high.astype(F32)).astype(BF16)


def memory_kernel(key_ref, value_ref, log_ref, out_ref):
    for head in range(HEADS_DEV):
        lanes = slice(head * HEAD_DIM, (head + 1) * HEAD_DIM)
        column, _ = cumulative_columns(log_ref[head : head + 1, :])
        last = column[TOK - 1 :, :]
        weighted = key_ref[:, lanes].astype(F32) * jnp.exp(last - column)
        high, low = split_bf16(weighted)
        value = value_ref[:, lanes]
        local = dot(high, value, 0, 0) + dot(low, value, 0, 0)
        pieces = slice(head * 16, (head + 1) * 16)
        total = jnp.broadcast_to(last, (8, HEAD_DIM))
        first, _ = split_bf16(total)
        second, third = split_bf16(total - first.astype(F32))
        sub = lax.broadcasted_iota(jnp.int32, (8, HEAD_DIM), 0)
        parts = jnp.where(
            sub == 0,
            first.astype(F32),
            jnp.where(sub == 1, second.astype(F32), jnp.where(sub == 2, third.astype(F32), 0.0)),
        )
        both = jnp.concatenate(
            [local.reshape(16, 8, HEAD_DIM), jnp.broadcast_to(parts[None], (16, 8, HEAD_DIM))],
            axis=1,
        )
        out_ref[pieces] = both.astype(BF16)


def scan_kernel(in_ref, out_ref, wide_ref):
    wide_ref[...] = in_ref[...].astype(F32)
    block_log = wide_ref[:, 8, :] + wide_ref[:, 9, :] + wide_ref[:, 10, :]
    row, col = iotas(SEGS)
    later = jnp.where(row > col, block_log, 0.0)
    trow = lax.broadcasted_iota(jnp.int32, (SEGS, SEGS), 0)
    tcol = lax.broadcasted_iota(jnp.int32, (SEGS, SEGS), 1)
    before = jnp.where(tcol < trow, 1.0, 0.0)
    spread = dot(before, later, 1, 0, lax.Precision.HIGHEST)[:, :SEGS]
    decay = jnp.where(tcol < trow, jnp.exp(spread), 0.0)
    high, low = split_bf16(decay)
    for sub in range(8):
        data = wide_ref[:, sub, :].astype(BF16)
        wide_ref[:, sub, :] = dot(high, data, 1, 0) + dot(low, data, 1, 0)
    out_ref[...] = wide_ref[:, 0:8, :].astype(BF16)


def inside_kernel(query_ref, key_ref, value_ref, log_ref, out_ref):
    row, col = iotas()
    for head in range(HEADS_DEV):
        lanes = slice(head * HEAD_DIM, (head + 1) * HEAD_DIM)
        column, as_row = cumulative_columns(log_ref[head : head + 1, :])
        scores = dot(query_ref[:, lanes], key_ref[:, lanes], 1, 1)
        causal = col <= row
        decay = jnp.exp(jnp.where(causal, column - as_row, 0.0))
        mixing = jnp.where(causal, scores * decay, 0.0).astype(BF16)
        out_ref[:, lanes] = dot(mixing, value_ref[:, lanes], 1, 0)


def mixed_kernel(query_ref, log_ref, inside_ref, memory_ref, out_ref, square_ref):
    row, col = iotas()
    squares = jnp.zeros((TOK, HEAD_DIM), F32)
    for head in range(HEADS_DEV):
        lanes = slice(head * HEAD_DIM, (head + 1) * HEAD_DIM)
        column, _ = cumulative_columns(log_ref[head : head + 1, :])
        memory = memory_ref[head * 16 : (head + 1) * 16].astype(F32).reshape(HEAD_DIM, HEAD_DIM)
        earlier = dot(query_ref[:, lanes], memory.astype(BF16), 1, 0)
        mixed = inside_ref[:, lanes] + jnp.exp(column) * earlier
        out_ref[:, lanes] = mixed
        squares = squares + mixed * mixed
    total = jnp.sum(squares, axis=1, keepdims=True)
    total_row = jnp.sum(jnp.where(row == col, total, 0.0), axis=0, keepdims=True)
    square_ref[...] = jnp.broadcast_to(total_row[None], square_ref.shape)


def gate_kernel(mixed_ref, square_ref, gain_ref, gate_ref, out_ref):
    row, col = iotas()
    shards = square_ref.shape[0]
    total_row = square_ref[0, 0:1, :]
    for shard in range(1, shards):
        total_row = total_row + square_ref[shard, 0:1, :]
    total = jnp.sum(jnp.where(row == col, total_row, 0.0), axis=1, keepdims=True)
    inverse = lax.rsqrt(total / (HEADS_DEV * HEAD_DIM * shards) + norm_eps)
    gated = mixed_ref[...] * inverse * gain_ref[...] * jax.nn.sigmoid(gate_ref[...].astype(F32))
    out_ref[...] = gated.astype(BF16)


def pieces_kernel(place_ref, key_ref, value_ref, out_ref):
    out_ref[:, :, 0:HEAD_DIM] = jnp.broadcast_to(key_ref[...][None], (ROWS, TOK, HEAD_DIM))
    out_ref[:, :, HEAD_DIM:] = jnp.broadcast_to(value_ref[...][None], (ROWS, TOK, HEAD_DIM))


def attend(place, core, seg_ref, own_segment, query_ref, pairs_ref, state):
    def block(step, state):
        column = jnp.bitwise_and(place // 2 - step, COLUMNS - 1)
        rows = pairs_ref[pl.ds(step * KEY_BLOCK, KEY_BLOCK)]
        keys = rows[:, :, 0:HEAD_DIM].reshape(KEY_BLOCK * TOK, HEAD_DIM)
        values = rows[:, :, HEAD_DIM:].reshape(KEY_BLOCK * TOK, HEAD_DIM)
        shift = []
        for at in range(KEY_BLOCK):
            seg = seg_ref[at * ROWS + column * 2 + core]
            shift.append(jnp.where(seg < own_segment, 0.0, MASKED).astype(F32))
        new_state = []
        for head in range(HEADS_DEV):
            peak, total, acc = state[head]
            query = query_ref[:, head * HEAD_DIM : (head + 1) * HEAD_DIM]
            logits = dot(query, keys, 1, 1)
            parts = [logits[:, at * TOK : (at + 1) * TOK] + shift[at] for at in range(KEY_BLOCK)]
            top = parts[0]
            for part in parts[1:]:
                top = jnp.maximum(top, part)
            new_peak = jnp.maximum(peak, jnp.max(top, axis=1, keepdims=True))
            fade = jnp.exp2((peak - new_peak) * (SCALE * LOG2E))
            weights = [jnp.exp2((part - new_peak) * (SCALE * LOG2E)) for part in parts]
            summed = weights[0]
            for part in weights[1:]:
                summed = summed + part
            low = jnp.concatenate([part.astype(BF16) for part in weights], axis=1)
            new_state.append(
                (new_peak, total * fade + summed, acc * fade + dot(low, values, 1, 0))
            )
        return tuple(new_state)

    return lax.fori_loop(0, HALF // KEY_BLOCK, block, state)


def first_kernel(
    seg_ref, place_ref, query_ref, own_ref, pairs_ref, acc_ref, total_ref, peak_ref
):
    place = place_ref[0]
    own_segment = seg_ref[place]
    row, col = iotas()
    keys = own_ref[0, :, 0:HEAD_DIM]
    values = own_ref[0, :, HEAD_DIM:]
    state = []
    for head in range(HEADS_DEV):
        query = query_ref[:, head * HEAD_DIM : (head + 1) * HEAD_DIM]
        logits = jnp.where(col <= row, dot(query, keys, 1, 1), MASKED)
        peak = jnp.max(logits, axis=1, keepdims=True)
        weights = jnp.exp2((logits - peak) * (SCALE * LOG2E))
        state.append((peak, weights, dot(weights.astype(BF16), values, 1, 0)))
    state = attend(place, place % 2, seg_ref, own_segment, query_ref, pairs_ref, tuple(state))
    for head in range(HEADS_DEV):
        peak, total, acc = state[head]
        acc_ref[head] = acc
        total_ref[head] = total
        peak_ref[head] = jnp.broadcast_to(peak, (TOK, HEAD_DIM))


def second_kernel(
    seg_ref, place_ref, query_ref, pairs_ref, acc_ref, total_ref, peak_ref, out_ref
):
    place = place_ref[0]
    own_segment = seg_ref[place]
    state = tuple(
        (peak_ref[head][:, 0:1], total_ref[head], acc_ref[head]) for head in range(HEADS_DEV)
    )
    state = attend(place, 1 - place % 2, seg_ref, own_segment, query_ref, pairs_ref, state)
    for head in range(HEADS_DEV):
        _, total, acc = state[head]
        lanes = slice(head * HEAD_DIM, (head + 1) * HEAD_DIM)
        out_ref[:, lanes] = (acc / jnp.sum(total, axis=1, keepdims=True)).astype(BF16)


def shape(*dims, dtype=F32):
    return jax.ShapeDtypeStruct(dims, dtype)


def local_memory(key, value, log_decay):
    return pl.pallas_call(
        memory_kernel, name="memory", out_shape=shape(SEGS, 16, HEAD_DIM, dtype=BF16),
        in_specs=[VM] * 3, out_specs=VM,
    )(key, value, log_decay)


def scan_memory(received):
    return pl.pallas_call(
        scan_kernel, name="scan", out_shape=shape(SEGS, 8, HEAD_DIM, dtype=BF16),
        in_specs=[VM], out_specs=VM, scratch_shapes=[pltpu.VMEM((SEGS, 16, HEAD_DIM), F32)],
    )(received)


def inside_part(query, key, value, log_decay):
    return pl.pallas_call(
        inside_kernel, name="inside", out_shape=shape(TOK, HEADS_DEV * HEAD_DIM),
        in_specs=[VM] * 4, out_specs=VM,
    )(query, key, value, log_decay)


def mixed_part(query, log_decay, inside, memory, shards):
    return pl.pallas_call(
        mixed_kernel, name="mixed",
        out_shape=(shape(TOK, HEADS_DEV * HEAD_DIM), shape(shards, 8, TOK)),
        in_specs=[VM] * 4, out_specs=(VM, VM),
    )(query, log_decay, inside, memory)


def gate_part(mixed, squares, gain, gate):
    return pl.pallas_call(
        gate_kernel, name="gate", out_shape=shape(TOK, HEADS_DEV * HEAD_DIM, dtype=BF16),
        in_specs=[VM] * 4, out_specs=VM,
    )(mixed, squares, gain[None, :], gate)


def key_value_pieces(place, key, value):
    return pl.pallas_call(
        pieces_kernel, name="pieces",
        out_shape=shape(ROWS, TOK, 2 * HEAD_DIM, dtype=BF16),
        grid_spec=pltpu.PrefetchScalarGridSpec(
            num_scalar_prefetch=1,
            grid=(1,),
            in_specs=[
                pl.BlockSpec((TOK, HEAD_DIM), lambda i, at: (0, at[0])),
                pl.BlockSpec((TOK, HEAD_DIM), lambda i, at: (0, at[0])),
            ],
            out_specs=pl.BlockSpec((ROWS, TOK, 2 * HEAD_DIM), lambda i, at: (0, 0, 0)),
        ),
    )(place, key, value)


def attend_first(segment_of, place, query, pieces, pairs):
    return pl.pallas_call(
        first_kernel, name="attend_first",
        out_shape=(shape(HEADS_DEV, TOK, HEAD_DIM),) * 3,
        grid=(1,),
        in_specs=[
            SM, SM,
            pl.BlockSpec((TOK, HEADS_DEV * HEAD_DIM), lambda i: (0, 0)),
            pl.BlockSpec((1, TOK, 2 * HEAD_DIM), lambda i: (0, 0, 0)),
            pl.BlockSpec((HALF, TOK, 2 * HEAD_DIM), lambda i: (0, 0, 0)),
        ],
        out_specs=(pl.BlockSpec((HEADS_DEV, TOK, HEAD_DIM), lambda i: (0, 0, 0)),) * 3,
    )(segment_of, place, query, pieces, pairs)


def attend_second(segment_of, place, query, pairs, state):
    return pl.pallas_call(
        second_kernel, name="attend_second",
        out_shape=shape(TOK, HEADS_DEV * HEAD_DIM, dtype=BF16),
        in_specs=[SM, SM] + [VM] * 5, out_specs=VM,
    )(segment_of, place, query, pairs, *state)


def shards(
    lin_query,
    lin_key,
    lin_value,
    log_decay,
    out_gate,
    norm_gain,
    soft_query,
    soft_key,
    soft_value,
    segment_of,
):
    place = lax.axis_index("seq").astype(jnp.int32)[None]
    shared = (lax.axis_index("head") * HEADS_DEV // Q_PER_KV).astype(jnp.int32)[None]
    head_shards = lax.axis_size("head")
    same_column = [[row * 8 + at for row in range(ROWS)] for at in range(8)]
    shifts = [
        [(at, at // 8 * 8 + (at + 2 * step) % 8) for at in range(SEGS)] for step in range(COLUMNS)
    ]
    partners = [(at, at ^ 1) for at in range(SEGS)]
    pieces = key_value_pieces(shared, soft_key, soft_value)
    column = lax.all_to_all(
        pieces, "seq", 0, 0, tiled=True, axis_index_groups=same_column
    )
    columns = [column] + [lax.ppermute(column, "seq", shifts[step]) for step in range(1, COLUMNS)]
    pairs = jnp.concatenate(columns, axis=0)
    local = local_memory(lin_key, lin_value, log_decay)
    received = lax.all_to_all(local, "seq", 0, 0, tiled=True)
    scanned = scan_memory(received)
    memory = lax.all_to_all(scanned, "seq", 0, 0, tiled=True)
    inside = inside_part(lin_query, lin_key, lin_value, log_decay)
    mixed, squares = mixed_part(lin_query, log_decay, inside, memory, head_shards)
    squares = lax.all_to_all(squares, "head", 0, 0, tiled=True)
    lin_out = gate_part(mixed, squares, norm_gain, out_gate)
    others = lax.ppermute(pairs, "seq", partners)
    state = attend_first(segment_of, place, soft_query, pieces, pairs)
    soft_out = attend_second(segment_of, place, soft_query, others, state)
    return (lin_out, soft_out)


def solution(mesh):
    return jax.shard_map(
        shards,
        mesh=mesh,
        in_specs=(
            P("seq", "head"),
            P("seq", "head"),
            P("seq", "head"),
            P("head", "seq"),
            P("seq", "head"),
            P("head"),
            P("seq", "head"),
            P("seq", None),
            P("seq", None),
            P(),
        ),
        out_specs=(P("seq", "head"), P("seq", "head")),
        check_vma=False,
    )
```

```python
import jax
import jax.numpy as jnp
from jax import lax
from jax.experimental import pallas as pl
from jax.experimental.pallas import tpu as pltpu
from jax.sharding import PartitionSpec as P


HEAD_DIM = 128
HEADS_DEV = 4
Q_PER_KV = 8
TOK = 128
SEGS = 64
ROWS = 8
COLUMNS = 4

norm_eps = 1e-06
SCALE = HEAD_DIM ** (-0.5)
LOG2E = 1.4426950408889634
F32 = jnp.float32
BF16 = jnp.bfloat16
MASKED = -1e30

VM = pl.BlockSpec(memory_space=pltpu.VMEM)
SM = pl.BlockSpec(memory_space=pltpu.SMEM)


def dot(a, b, ca, cb, precision=None):
    return lax.dot_general(
        a, b, (((ca,), (cb,)), ((), ())), precision=precision, preferred_element_type=F32
    )


def iotas(n=TOK):
    return (
        lax.broadcasted_iota(jnp.int32, (n, TOK), 0),
        lax.broadcasted_iota(jnp.int32, (n, TOK), 1),
    )


def cumulative_columns(log_row):
    row, col = iotas()
    wide = jnp.broadcast_to(log_row, (TOK, TOK))
    column = jnp.sum(jnp.where(col <= row, wide, 0.0), axis=1, keepdims=True)
    log_column = jnp.sum(jnp.where(col == row, wide, 0.0), axis=1, keepdims=True)
    as_row = jnp.sum(jnp.where(row <= col, log_column, 0.0), axis=0, keepdims=True)
    return column, as_row


def split_bf16(value):
    high = value.astype(BF16)
    return high, (value - high.astype(F32)).astype(BF16)


def memory_kernel(key_ref, value_ref, log_ref, out_ref):
    for head in range(HEADS_DEV):
        lanes = slice(head * HEAD_DIM, (head + 1) * HEAD_DIM)
        column, _ = cumulative_columns(log_ref[head : head + 1, :])
        last = column[TOK - 1 :, :]
        weighted = key_ref[:, lanes].astype(F32) * jnp.exp(last - column)
        high, low = split_bf16(weighted)
        value = value_ref[:, lanes]
        local = dot(high, value, 0, 0) + dot(low, value, 0, 0)
        pieces = slice(head * 16, (head + 1) * 16)
        total = jnp.broadcast_to(last, (8, HEAD_DIM))
        first, _ = split_bf16(total)
        second, third = split_bf16(total - first.astype(F32))
        sub = lax.broadcasted_iota(jnp.int32, (8, HEAD_DIM), 0)
        parts = jnp.where(
            sub == 0,
            first.astype(F32),
            jnp.where(sub == 1, second.astype(F32), jnp.where(sub == 2, third.astype(F32), 0.0)),
        )
        both = jnp.concatenate(
            [local.reshape(16, 8, HEAD_DIM), jnp.broadcast_to(parts[None], (16, 8, HEAD_DIM))],
            axis=1,
        )
        out_ref[pieces] = both.astype(BF16)


def scan_kernel(in_ref, out_ref, wide_ref):
    wide_ref[...] = in_ref[...].astype(F32)
    block_log = wide_ref[:, 8, :] + wide_ref[:, 9, :] + wide_ref[:, 10, :]
    row, col = iotas(SEGS)
    later = jnp.where(row > col, block_log, 0.0)
    trow = lax.broadcasted_iota(jnp.int32, (SEGS, SEGS), 0)
    tcol = lax.broadcasted_iota(jnp.int32, (SEGS, SEGS), 1)
    before = jnp.where(tcol < trow, 1.0, 0.0)
    spread = dot(before, later, 1, 0, lax.Precision.HIGHEST)[:, :SEGS]
    decay = jnp.where(tcol < trow, jnp.exp(spread), 0.0)
    high, low = split_bf16(decay)
    for sub in range(8):
        data = wide_ref[:, sub, :].astype(BF16)
        wide_ref[:, sub, :] = dot(high, data, 1, 0) + dot(low, data, 1, 0)
    out_ref[...] = wide_ref[:, 0:8, :].astype(BF16)


def inside_kernel(query_ref, key_ref, value_ref, log_ref, out_ref):
    row, col = iotas()
    for head in range(HEADS_DEV):
        lanes = slice(head * HEAD_DIM, (head + 1) * HEAD_DIM)
        column, as_row = cumulative_columns(log_ref[head : head + 1, :])
        scores = dot(query_ref[:, lanes], key_ref[:, lanes], 1, 1)
        causal = col <= row
        decay = jnp.exp(jnp.where(causal, column - as_row, 0.0))
        mixing = jnp.where(causal, scores * decay, 0.0).astype(BF16)
        out_ref[:, lanes] = dot(mixing, value_ref[:, lanes], 1, 0)


def mixed_kernel(query_ref, log_ref, inside_ref, memory_ref, out_ref, square_ref):
    row, col = iotas()
    squares = jnp.zeros((TOK, HEAD_DIM), F32)
    for head in range(HEADS_DEV):
        lanes = slice(head * HEAD_DIM, (head + 1) * HEAD_DIM)
        column, _ = cumulative_columns(log_ref[head : head + 1, :])
        memory = memory_ref[head * 16 : (head + 1) * 16].astype(F32).reshape(HEAD_DIM, HEAD_DIM)
        earlier = dot(query_ref[:, lanes], memory.astype(BF16), 1, 0)
        mixed = inside_ref[:, lanes] + jnp.exp(column) * earlier
        out_ref[:, lanes] = mixed
        squares = squares + mixed * mixed
    total = jnp.sum(squares, axis=1, keepdims=True)
    total_row = jnp.sum(jnp.where(row == col, total, 0.0), axis=0, keepdims=True)
    square_ref[...] = jnp.broadcast_to(total_row[None], square_ref.shape)


def gate_kernel(mixed_ref, square_ref, gain_ref, gate_ref, out_ref):
    row, col = iotas()
    shards = square_ref.shape[0]
    total_row = square_ref[0, 0:1, :]
    for shard in range(1, shards):
        total_row = total_row + square_ref[shard, 0:1, :]
    total = jnp.sum(jnp.where(row == col, total_row, 0.0), axis=1, keepdims=True)
    inverse = lax.rsqrt(total / (HEADS_DEV * HEAD_DIM * shards) + norm_eps)
    gated = mixed_ref[...] * inverse * gain_ref[...] * jax.nn.sigmoid(gate_ref[...].astype(F32))
    out_ref[...] = gated.astype(BF16)


def pieces_kernel(place_ref, key_ref, value_ref, out_ref):
    out_ref[:, :, 0:HEAD_DIM] = jnp.broadcast_to(key_ref[...][None], (ROWS, TOK, HEAD_DIM))
    out_ref[:, :, HEAD_DIM:] = jnp.broadcast_to(value_ref[...][None], (ROWS, TOK, HEAD_DIM))


def stack_heads(query_ref, heads_ref):
    for head in range(HEADS_DEV):
        heads_ref[head * TOK : (head + 1) * TOK] = query_ref[:, head * HEAD_DIM : (head + 1) * HEAD_DIM]


def score_columns(pairs_ref, columns, core, place, seg_ref, heads_ref, score_ref, top_ref):
    own_segment = seg_ref[place]

    def score(column, carry):
        source = jnp.bitwise_and(place // 2 - column, COLUMNS - 1)
        keys = pairs_ref[pl.ds(column * ROWS, ROWS), :, 0:HEAD_DIM].reshape(ROWS * TOK, HEAD_DIM)
        logits = dot(heads_ref[...], keys, 1, 1)
        top = top_ref[...]
        for at in range(ROWS):
            seg = seg_ref[at * ROWS + source * 2 + core]
            part = logits[:, at * TOK : (at + 1) * TOK] + jnp.where(seg < own_segment, 0.0, MASKED).astype(F32)
            top = jnp.maximum(top, part)
            score_ref[column - columns[0], :, at * TOK : (at + 1) * TOK] = part
        top_ref[...] = top
        return carry

    lax.fori_loop(*columns, score, 0)


def weigh_columns(pairs_ref, columns, score_ref, peak_ref, total_ref, acc_ref):
    def weigh(column, carry):
        values = pairs_ref[pl.ds(column * ROWS, ROWS), :, HEAD_DIM:].reshape(ROWS * TOK, HEAD_DIM)
        peak = peak_ref[...]
        total = total_ref[...]
        low = []
        for at in range(ROWS):
            part = score_ref[column - columns[0], :, at * TOK : (at + 1) * TOK]
            weights = jnp.exp2((part - peak) * (SCALE * LOG2E))
            total = total + weights
            low.append(weights.astype(BF16))
        total_ref[...] = total
        acc_ref[...] += dot(jnp.concatenate(low, axis=1), values, 1, 0)
        return carry

    lax.fori_loop(*columns, weigh, 0)


def widest(top):
    return jnp.broadcast_to(jnp.max(top, axis=1, keepdims=True), top.shape)


def own_kernel(
    seg_ref, place_ref, query_ref, own_ref, column_ref,
    peak_ref, total_ref, acc_ref, heads_ref, score_ref, own_score_ref,
):
    place = place_ref[0]
    stack_heads(query_ref, heads_ref)
    row = jnp.bitwise_and(lax.broadcasted_iota(jnp.int32, (HEADS_DEV * TOK, TOK), 0), TOK - 1)
    col = lax.broadcasted_iota(jnp.int32, (HEADS_DEV * TOK, TOK), 1)
    logits = jnp.where(col <= row, dot(heads_ref[...], own_ref[0, :, 0:HEAD_DIM], 1, 1), MASKED)
    own_score_ref[...] = logits
    peak_ref[...] = logits
    score_columns(column_ref, (0, 1), place % 2, place, seg_ref, heads_ref, score_ref, peak_ref)
    peak_ref[...] = widest(peak_ref[...])
    weights = jnp.exp2((own_score_ref[...] - peak_ref[...]) * (SCALE * LOG2E))
    total_ref[...] = weights
    acc_ref[...] = dot(weights.astype(BF16), own_ref[0, :, HEAD_DIM:], 1, 0)
    weigh_columns(column_ref, (0, 1), score_ref, peak_ref, total_ref, acc_ref)


def later_columns(pairs_ref, columns, core, seg_ref, place, query_ref, old, new, scratch):
    heads_ref, score_ref = scratch
    old_peak_ref, old_total_ref, old_acc_ref = old
    peak_ref, total_ref, acc_ref = new
    stack_heads(query_ref, heads_ref)
    peak_ref[...] = old_peak_ref[...]
    score_columns(pairs_ref, columns, core, place, seg_ref, heads_ref, score_ref, peak_ref)
    peak = widest(peak_ref[...])
    peak_ref[...] = peak
    fade = jnp.exp2((old_peak_ref[...] - peak) * (SCALE * LOG2E))
    total_ref[...] = old_total_ref[...] * fade
    acc_ref[...] = old_acc_ref[...] * fade
    weigh_columns(pairs_ref, columns, score_ref, peak_ref, total_ref, acc_ref)


def shifted_kernel(
    seg_ref, place_ref, query_ref, pairs_ref,
    old_peak_ref, old_total_ref, old_acc_ref,
    peak_ref, total_ref, acc_ref, heads_ref, score_ref,
):
    place = place_ref[0]
    later_columns(
        pairs_ref, (1, COLUMNS), place % 2, seg_ref, place, query_ref,
        (old_peak_ref, old_total_ref, old_acc_ref), (peak_ref, total_ref, acc_ref),
        (heads_ref, score_ref),
    )


def swapped_kernel(
    seg_ref, place_ref, query_ref, pairs_ref,
    old_peak_ref, old_total_ref, old_acc_ref,
    out_ref, peak_ref, total_ref, acc_ref, heads_ref, score_ref,
):
    place = place_ref[0]
    later_columns(
        pairs_ref, (0, COLUMNS), 1 - place % 2, seg_ref, place, query_ref,
        (old_peak_ref, old_total_ref, old_acc_ref), (peak_ref, total_ref, acc_ref),
        (heads_ref, score_ref),
    )
    for head in range(HEADS_DEV):
        rows = slice(head * TOK, (head + 1) * TOK)
        total = jnp.sum(total_ref[rows], axis=1, keepdims=True)
        out_ref[:, head * HEAD_DIM : (head + 1) * HEAD_DIM] = (acc_ref[rows] / total).astype(BF16)


def shape(*dims, dtype=F32):
    return jax.ShapeDtypeStruct(dims, dtype)


def local_memory(key, value, log_decay):
    return pl.pallas_call(
        memory_kernel, name="memory", out_shape=shape(SEGS, 16, HEAD_DIM, dtype=BF16),
        in_specs=[VM] * 3, out_specs=VM,
    )(key, value, log_decay)


def scan_memory(received):
    return pl.pallas_call(
        scan_kernel, name="scan", out_shape=shape(SEGS, 8, HEAD_DIM, dtype=BF16),
        in_specs=[VM], out_specs=VM, scratch_shapes=[pltpu.VMEM((SEGS, 16, HEAD_DIM), F32)],
    )(received)


def inside_part(query, key, value, log_decay):
    return pl.pallas_call(
        inside_kernel, name="inside", out_shape=shape(TOK, HEADS_DEV * HEAD_DIM),
        in_specs=[VM] * 4, out_specs=VM,
    )(query, key, value, log_decay)


def mixed_part(query, log_decay, inside, memory, shards):
    return pl.pallas_call(
        mixed_kernel, name="mixed",
        out_shape=(shape(TOK, HEADS_DEV * HEAD_DIM), shape(shards, 8, TOK)),
        in_specs=[VM] * 4, out_specs=(VM, VM),
    )(query, log_decay, inside, memory)


def gate_part(mixed, squares, gain, gate):
    return pl.pallas_call(
        gate_kernel, name="gate", out_shape=shape(TOK, HEADS_DEV * HEAD_DIM, dtype=BF16),
        in_specs=[VM] * 4, out_specs=VM,
    )(mixed, squares, gain[None, :], gate)


def key_value_pieces(place, key, value):
    return pl.pallas_call(
        pieces_kernel, name="pieces",
        out_shape=shape(ROWS, TOK, 2 * HEAD_DIM, dtype=BF16),
        grid_spec=pltpu.PrefetchScalarGridSpec(
            num_scalar_prefetch=1,
            grid=(1,),
            in_specs=[
                pl.BlockSpec((TOK, HEAD_DIM), lambda i, at: (0, at[0])),
                pl.BlockSpec((TOK, HEAD_DIM), lambda i, at: (0, at[0])),
            ],
            out_specs=pl.BlockSpec((ROWS, TOK, 2 * HEAD_DIM), lambda i, at: (0, 0, 0)),
        ),
    )(place, key, value)


STACKED = HEADS_DEV * TOK


def state_scratch(count):
    return [pltpu.VMEM((STACKED, HEAD_DIM), F32)] * count


def score_scratch(columns):
    return [
        pltpu.VMEM((STACKED, HEAD_DIM), BF16),
        pltpu.VMEM((columns, STACKED, ROWS * TOK), F32),
    ]


def attend_own(segment_of, place, query, pieces, column):
    whole = lambda *dims: pl.BlockSpec(dims, lambda i: (0,) * len(dims))
    return pl.pallas_call(
        own_kernel, name="own",
        out_shape=(shape(STACKED, HEAD_DIM),) * 3,
        grid=(1,),
        in_specs=[
            SM, SM, whole(TOK, HEADS_DEV * HEAD_DIM), whole(1, TOK, 2 * HEAD_DIM),
            whole(ROWS, TOK, 2 * HEAD_DIM),
        ],
        out_specs=(whole(STACKED, HEAD_DIM),) * 3,
        scratch_shapes=score_scratch(1) + state_scratch(1),
    )(segment_of, place, query, pieces, column)


def attend_shifted(segment_of, place, query, pairs, state):
    return pl.pallas_call(
        shifted_kernel, name="shifted",
        out_shape=(shape(STACKED, HEAD_DIM),) * 3,
        in_specs=[SM, SM] + [VM] * 5, out_specs=(VM,) * 3,
        scratch_shapes=score_scratch(COLUMNS - 1),
    )(segment_of, place, query, pairs, *state)


def attend_swapped(segment_of, place, query, pairs, state):
    return pl.pallas_call(
        swapped_kernel, name="swapped",
        out_shape=shape(TOK, HEADS_DEV * HEAD_DIM, dtype=BF16),
        in_specs=[SM, SM] + [VM] * 5, out_specs=VM,
        scratch_shapes=state_scratch(3) + score_scratch(COLUMNS),
    )(segment_of, place, query, pairs, *state)


def shards(
    lin_query,
    lin_key,
    lin_value,
    log_decay,
    out_gate,
    norm_gain,
    soft_query,
    soft_key,
    soft_value,
    segment_of,
):
    place = lax.axis_index("seq").astype(jnp.int32)[None]
    shared = (lax.axis_index("head") * HEADS_DEV // Q_PER_KV).astype(jnp.int32)[None]
    head_shards = lax.axis_size("head")
    same_column = [[row * 8 + at for row in range(ROWS)] for at in range(8)]
    shifts = [
        [(at, at // 8 * 8 + (at + 2 * step) % 8) for at in range(SEGS)] for step in range(COLUMNS)
    ]
    partners = [(at, at ^ 1) for at in range(SEGS)]
    pieces = key_value_pieces(shared, soft_key, soft_value)
    column = lax.all_to_all(
        pieces, "seq", 0, 0, tiled=True, axis_index_groups=same_column
    )
    columns = [column] + [lax.ppermute(column, "seq", shifts[step]) for step in range(1, COLUMNS)]
    pairs = jnp.concatenate(columns, axis=0)
    local = local_memory(lin_key, lin_value, log_decay)
    received = lax.all_to_all(local, "seq", 0, 0, tiled=True)
    scanned = scan_memory(received)
    memory = lax.all_to_all(scanned, "seq", 0, 0, tiled=True)
    inside = inside_part(lin_query, lin_key, lin_value, log_decay)
    mixed, squares = mixed_part(lin_query, log_decay, inside, memory, head_shards)
    squares = lax.all_to_all(squares, "head", 0, 0, tiled=True)
    lin_out = gate_part(mixed, squares, norm_gain, out_gate)
    others = lax.ppermute(pairs, "seq", partners)
    state = attend_own(segment_of, place, soft_query, pieces, column)
    state = attend_shifted(segment_of, place, soft_query, pairs, state)
    soft_out = attend_swapped(segment_of, place, soft_query, others, state)
    return (lin_out, soft_out)


def solution(mesh):
    return jax.shard_map(
        shards,
        mesh=mesh,
        in_specs=(
            P("seq", "head"),
            P("seq", "head"),
            P("seq", "head"),
            P("head", "seq"),
            P("seq", "head"),
            P("head"),
            P("seq", "head"),
            P("seq", None),
            P("seq", None),
            P(),
        ),
        out_specs=(P("seq", "head"), P("seq", "head")),
        check_vma=False,
    )
```

```python
import jax
import jax.numpy as jnp
from jax import lax
from jax.experimental import pallas as pl
from jax.experimental.pallas import tpu as pltpu
from jax.sharding import PartitionSpec as P


HEAD_DIM = 128
HEADS_DEV = 4
Q_PER_KV = 8
TOK = 128
SEGS = 64
HALF = 32
ROWS = 8
COLUMNS = 4

norm_eps = 1e-06
SCALE = HEAD_DIM ** (-0.5)
LOG2E = 1.4426950408889634
F32 = jnp.float32
BF16 = jnp.bfloat16
MASKED = -1e30
VMEM_GRANT = 64 * 1024 * 1024

VM = pl.BlockSpec(memory_space=pltpu.VMEM)
SM = pl.BlockSpec(memory_space=pltpu.SMEM)


def dot(a, b, ca, cb, precision=None):
    return lax.dot_general(
        a, b, (((ca,), (cb,)), ((), ())), precision=precision, preferred_element_type=F32
    )


def iotas(n=TOK):
    return (
        lax.broadcasted_iota(jnp.int32, (n, TOK), 0),
        lax.broadcasted_iota(jnp.int32, (n, TOK), 1),
    )


def cumulative_columns(log_row):
    row, col = iotas()
    wide = jnp.broadcast_to(log_row, (TOK, TOK))
    column = jnp.sum(jnp.where(col <= row, wide, 0.0), axis=1, keepdims=True)
    log_column = jnp.sum(jnp.where(col == row, wide, 0.0), axis=1, keepdims=True)
    as_row = jnp.sum(jnp.where(row <= col, log_column, 0.0), axis=0, keepdims=True)
    return column, as_row


def split_bf16(value):
    high = value.astype(BF16)
    return high, (value - high.astype(F32)).astype(BF16)


def memory_kernel(key_ref, value_ref, log_ref, out_ref):
    for head in range(HEADS_DEV):
        lanes = slice(head * HEAD_DIM, (head + 1) * HEAD_DIM)
        column, _ = cumulative_columns(log_ref[head : head + 1, :])
        last = column[TOK - 1 :, :]
        weighted = key_ref[:, lanes].astype(F32) * jnp.exp(last - column)
        high, low = split_bf16(weighted)
        value = value_ref[:, lanes]
        local = dot(high, value, 0, 0) + dot(low, value, 0, 0)
        pieces = slice(head * 16, (head + 1) * 16)
        total = jnp.broadcast_to(last, (8, HEAD_DIM))
        first, _ = split_bf16(total)
        second, third = split_bf16(total - first.astype(F32))
        sub = lax.broadcasted_iota(jnp.int32, (8, HEAD_DIM), 0)
        parts = jnp.where(
            sub == 0,
            first.astype(F32),
            jnp.where(sub == 1, second.astype(F32), jnp.where(sub == 2, third.astype(F32), 0.0)),
        )
        both = jnp.concatenate(
            [local.reshape(16, 8, HEAD_DIM), jnp.broadcast_to(parts[None], (16, 8, HEAD_DIM))],
            axis=1,
        )
        out_ref[pieces] = both.astype(BF16)


def scan_kernel(in_ref, out_ref, wide_ref):
    wide_ref[...] = in_ref[...].astype(F32)
    block_log = wide_ref[:, 8, :] + wide_ref[:, 9, :] + wide_ref[:, 10, :]
    row, col = iotas(SEGS)
    later = jnp.where(row > col, block_log, 0.0)
    trow = lax.broadcasted_iota(jnp.int32, (SEGS, SEGS), 0)
    tcol = lax.broadcasted_iota(jnp.int32, (SEGS, SEGS), 1)
    before = jnp.where(tcol < trow, 1.0, 0.0)
    spread = dot(before, later, 1, 0, lax.Precision.HIGHEST)[:, :SEGS]
    decay = jnp.where(tcol < trow, jnp.exp(spread), 0.0)
    high, low = split_bf16(decay)
    for sub in range(8):
        data = wide_ref[:, sub, :].astype(BF16)
        wide_ref[:, sub, :] = dot(high, data, 1, 0) + dot(low, data, 1, 0)
    out_ref[...] = wide_ref[:, 0:8, :].astype(BF16)


def inside_kernel(query_ref, key_ref, value_ref, log_ref, out_ref):
    row, col = iotas()
    for head in range(HEADS_DEV):
        lanes = slice(head * HEAD_DIM, (head + 1) * HEAD_DIM)
        column, as_row = cumulative_columns(log_ref[head : head + 1, :])
        scores = dot(query_ref[:, lanes], key_ref[:, lanes], 1, 1)
        causal = col <= row
        decay = jnp.exp(jnp.where(causal, column - as_row, 0.0))
        mixing = jnp.where(causal, scores * decay, 0.0).astype(BF16)
        out_ref[:, lanes] = dot(mixing, value_ref[:, lanes], 1, 0)


def mixed_kernel(query_ref, log_ref, inside_ref, memory_ref, out_ref, square_ref):
    row, col = iotas()
    squares = jnp.zeros((TOK, HEAD_DIM), F32)
    for head in range(HEADS_DEV):
        lanes = slice(head * HEAD_DIM, (head + 1) * HEAD_DIM)
        column, _ = cumulative_columns(log_ref[head : head + 1, :])
        memory = memory_ref[head * 16 : (head + 1) * 16].astype(F32).reshape(HEAD_DIM, HEAD_DIM)
        earlier = dot(query_ref[:, lanes], memory.astype(BF16), 1, 0)
        mixed = inside_ref[:, lanes] + jnp.exp(column) * earlier
        out_ref[:, lanes] = mixed
        squares = squares + mixed * mixed
    total = jnp.sum(squares, axis=1, keepdims=True)
    total_row = jnp.sum(jnp.where(row == col, total, 0.0), axis=0, keepdims=True)
    square_ref[...] = jnp.broadcast_to(total_row[None], square_ref.shape)


def gate_kernel(mixed_ref, square_ref, gain_ref, gate_ref, out_ref):
    row, col = iotas()
    shards = square_ref.shape[0]
    total_row = square_ref[0, 0:1, :]
    for shard in range(1, shards):
        total_row = total_row + square_ref[shard, 0:1, :]
    total = jnp.sum(jnp.where(row == col, total_row, 0.0), axis=1, keepdims=True)
    inverse = lax.rsqrt(total / (HEADS_DEV * HEAD_DIM * shards) + norm_eps)
    gated = mixed_ref[...] * inverse * gain_ref[...] * jax.nn.sigmoid(gate_ref[...].astype(F32))
    out_ref[...] = gated.astype(BF16)


def pieces_kernel(place_ref, key_ref, value_ref, out_ref):
    out_ref[:, :, 0:HEAD_DIM] = jnp.broadcast_to(key_ref[...][None], (ROWS, TOK, HEAD_DIM))
    out_ref[:, :, HEAD_DIM:] = jnp.broadcast_to(value_ref[...][None], (ROWS, TOK, HEAD_DIM))


def stack_heads(query_ref, heads_ref):
    for head in range(HEADS_DEV):
        heads_ref[head * TOK : (head + 1) * TOK] = query_ref[:, head * HEAD_DIM : (head + 1) * HEAD_DIM]


def score_columns(pairs_ref, columns, core, place, seg_ref, heads_ref, score_ref, top_ref):
    own_segment = seg_ref[place]

    def score(column, carry):
        source = jnp.bitwise_and(place // 2 - column, COLUMNS - 1)
        keys = pairs_ref[pl.ds(column * ROWS, ROWS), :, 0:HEAD_DIM].reshape(ROWS * TOK, HEAD_DIM)
        logits = dot(heads_ref[...], keys, 1, 1)
        top = top_ref[...]
        for at in range(ROWS):
            seg = seg_ref[at * ROWS + source * 2 + core]
            part = logits[:, at * TOK : (at + 1) * TOK] + jnp.where(seg < own_segment, 0.0, MASKED).astype(F32)
            top = jnp.maximum(top, part)
            score_ref[column - columns[0], :, at * TOK : (at + 1) * TOK] = part
        top_ref[...] = top
        return carry

    lax.fori_loop(*columns, score, 0)


def weigh_columns(pairs_ref, columns, score_ref, peak_ref, total_ref, acc_ref):
    def weigh(column, carry):
        values = pairs_ref[pl.ds(column * ROWS, ROWS), :, HEAD_DIM:].reshape(ROWS * TOK, HEAD_DIM)
        peak = peak_ref[...]
        total = total_ref[...]
        low = []
        for at in range(ROWS):
            part = score_ref[column - columns[0], :, at * TOK : (at + 1) * TOK]
            weights = jnp.exp2((part - peak) * (SCALE * LOG2E))
            total = total + weights
            low.append(weights.astype(BF16))
        total_ref[...] = total
        acc_ref[...] += dot(jnp.concatenate(low, axis=1), values, 1, 0)
        return carry

    lax.fori_loop(*columns, weigh, 0)


def widest(top):
    return jnp.broadcast_to(jnp.max(top, axis=1, keepdims=True), top.shape)


def own_kernel(
    seg_ref, place_ref, query_ref, own_ref, column_ref,
    peak_ref, total_ref, acc_ref, heads_ref, score_ref, own_score_ref,
):
    place = place_ref[0]
    stack_heads(query_ref, heads_ref)
    row = jnp.bitwise_and(lax.broadcasted_iota(jnp.int32, (HEADS_DEV * TOK, TOK), 0), TOK - 1)
    col = lax.broadcasted_iota(jnp.int32, (HEADS_DEV * TOK, TOK), 1)
    logits = jnp.where(col <= row, dot(heads_ref[...], own_ref[0, :, 0:HEAD_DIM], 1, 1), MASKED)
    own_score_ref[...] = logits
    peak_ref[...] = logits
    score_columns(column_ref, (0, 1), place % 2, place, seg_ref, heads_ref, score_ref, peak_ref)
    peak_ref[...] = widest(peak_ref[...])
    weights = jnp.exp2((own_score_ref[...] - peak_ref[...]) * (SCALE * LOG2E))
    total_ref[...] = weights
    acc_ref[...] = dot(weights.astype(BF16), own_ref[0, :, HEAD_DIM:], 1, 0)
    weigh_columns(column_ref, (0, 1), score_ref, peak_ref, total_ref, acc_ref)


def later_columns(pairs_ref, columns, core, seg_ref, place, query_ref, old, new, scratch):
    heads_ref, score_ref = scratch
    old_peak_ref, old_total_ref, old_acc_ref = old
    peak_ref, total_ref, acc_ref = new
    stack_heads(query_ref, heads_ref)
    peak_ref[...] = old_peak_ref[...]
    score_columns(pairs_ref, columns, core, place, seg_ref, heads_ref, score_ref, peak_ref)
    peak = widest(peak_ref[...])
    peak_ref[...] = peak
    fade = jnp.exp2((old_peak_ref[...] - peak) * (SCALE * LOG2E))
    total_ref[...] = old_total_ref[...] * fade
    acc_ref[...] = old_acc_ref[...] * fade
    weigh_columns(pairs_ref, columns, score_ref, peak_ref, total_ref, acc_ref)


def shifted_kernel(
    seg_ref, place_ref, query_ref, zero_ref, one_ref, two_ref, three_ref,
    old_peak_ref, old_total_ref, old_acc_ref,
    peak_ref, total_ref, acc_ref, pairs_ref, heads_ref, score_ref,
):
    place = place_ref[0]
    for column, column_ref in enumerate((zero_ref, one_ref, two_ref, three_ref)):
        pairs_ref[column * ROWS : (column + 1) * ROWS] = column_ref[...]
    later_columns(
        pairs_ref, (1, COLUMNS), place % 2, seg_ref, place, query_ref,
        (old_peak_ref, old_total_ref, old_acc_ref), (peak_ref, total_ref, acc_ref),
        (heads_ref, score_ref),
    )


def swapped_kernel(
    seg_ref, place_ref, query_ref, pairs_ref,
    old_peak_ref, old_total_ref, old_acc_ref,
    out_ref, peak_ref, total_ref, acc_ref, heads_ref, score_ref,
):
    place = place_ref[0]
    later_columns(
        pairs_ref, (0, COLUMNS), 1 - place % 2, seg_ref, place, query_ref,
        (old_peak_ref, old_total_ref, old_acc_ref), (peak_ref, total_ref, acc_ref),
        (heads_ref, score_ref),
    )
    for head in range(HEADS_DEV):
        rows = slice(head * TOK, (head + 1) * TOK)
        total = jnp.sum(total_ref[rows], axis=1, keepdims=True)
        out_ref[:, head * HEAD_DIM : (head + 1) * HEAD_DIM] = (acc_ref[rows] / total).astype(BF16)


def shape(*dims, dtype=F32):
    return jax.ShapeDtypeStruct(dims, dtype)


def local_memory(key, value, log_decay):
    return pl.pallas_call(
        memory_kernel, name="memory", compiler_params=pltpu.CompilerParams(vmem_limit_bytes=VMEM_GRANT), out_shape=shape(SEGS, 16, HEAD_DIM, dtype=BF16),
        in_specs=[VM] * 3, out_specs=VM,
    )(key, value, log_decay)


def scan_memory(received):
    return pl.pallas_call(
        scan_kernel, name="scan", compiler_params=pltpu.CompilerParams(vmem_limit_bytes=VMEM_GRANT), out_shape=shape(SEGS, 8, HEAD_DIM, dtype=BF16),
        in_specs=[VM], out_specs=VM, scratch_shapes=[pltpu.VMEM((SEGS, 16, HEAD_DIM), F32)],
    )(received)


def inside_part(query, key, value, log_decay):
    return pl.pallas_call(
        inside_kernel, name="inside", compiler_params=pltpu.CompilerParams(vmem_limit_bytes=VMEM_GRANT), out_shape=shape(TOK, HEADS_DEV * HEAD_DIM),
        in_specs=[VM] * 4, out_specs=VM,
    )(query, key, value, log_decay)


def mixed_part(query, log_decay, inside, memory, shards):
    return pl.pallas_call(
        mixed_kernel, name="mixed", compiler_params=pltpu.CompilerParams(vmem_limit_bytes=VMEM_GRANT),
        out_shape=(shape(TOK, HEADS_DEV * HEAD_DIM), shape(shards, 8, TOK)),
        in_specs=[VM] * 4, out_specs=(VM, VM),
    )(query, log_decay, inside, memory)


def gate_part(mixed, squares, gain, gate):
    return pl.pallas_call(
        gate_kernel, name="gate", compiler_params=pltpu.CompilerParams(vmem_limit_bytes=VMEM_GRANT), out_shape=shape(TOK, HEADS_DEV * HEAD_DIM, dtype=BF16),
        in_specs=[VM] * 4, out_specs=VM,
    )(mixed, squares, gain[None, :], gate)


def key_value_pieces(place, key, value):
    return pl.pallas_call(
        pieces_kernel, name="pieces", compiler_params=pltpu.CompilerParams(vmem_limit_bytes=VMEM_GRANT),
        out_shape=shape(ROWS, TOK, 2 * HEAD_DIM, dtype=BF16),
        grid_spec=pltpu.PrefetchScalarGridSpec(
            num_scalar_prefetch=1,
            grid=(1,),
            in_specs=[
                pl.BlockSpec((TOK, HEAD_DIM), lambda i, at: (0, at[0])),
                pl.BlockSpec((TOK, HEAD_DIM), lambda i, at: (0, at[0])),
            ],
            out_specs=pl.BlockSpec((ROWS, TOK, 2 * HEAD_DIM), lambda i, at: (0, 0, 0)),
        ),
    )(place, key, value)


STACKED = HEADS_DEV * TOK


def state_scratch(count):
    return [pltpu.VMEM((STACKED, HEAD_DIM), F32)] * count


def score_scratch(columns):
    return [
        pltpu.VMEM((STACKED, HEAD_DIM), BF16),
        pltpu.VMEM((columns, STACKED, ROWS * TOK), F32),
    ]


def attend_own(segment_of, place, query, pieces, column):
    whole = lambda *dims: pl.BlockSpec(dims, lambda i: (0,) * len(dims))
    return pl.pallas_call(
        own_kernel, name="own", compiler_params=pltpu.CompilerParams(vmem_limit_bytes=VMEM_GRANT),
        out_shape=(shape(STACKED, HEAD_DIM),) * 3,
        grid=(1,),
        in_specs=[
            SM, SM, whole(TOK, HEADS_DEV * HEAD_DIM), whole(1, TOK, 2 * HEAD_DIM),
            whole(ROWS, TOK, 2 * HEAD_DIM),
        ],
        out_specs=(whole(STACKED, HEAD_DIM),) * 3,
        scratch_shapes=score_scratch(1) + state_scratch(1),
    )(segment_of, place, query, pieces, column)


def attend_shifted(segment_of, place, query, columns, state):
    return pl.pallas_call(
        shifted_kernel, name="shifted", compiler_params=pltpu.CompilerParams(vmem_limit_bytes=VMEM_GRANT),
        out_shape=(shape(STACKED, HEAD_DIM),) * 3 + (shape(HALF, TOK, 2 * HEAD_DIM, dtype=BF16),),
        in_specs=[SM, SM] + [VM] * 8, out_specs=(VM,) * 4,
        scratch_shapes=score_scratch(COLUMNS - 1),
    )(segment_of, place, query, *columns, *state)


def attend_swapped(segment_of, place, query, pairs, state):
    return pl.pallas_call(
        swapped_kernel, name="swapped", compiler_params=pltpu.CompilerParams(vmem_limit_bytes=VMEM_GRANT),
        out_shape=shape(TOK, HEADS_DEV * HEAD_DIM, dtype=BF16),
        in_specs=[SM, SM] + [VM] * 5, out_specs=VM,
        scratch_shapes=state_scratch(3) + score_scratch(COLUMNS),
    )(segment_of, place, query, pairs, *state)


def shards(
    lin_query,
    lin_key,
    lin_value,
    log_decay,
    out_gate,
    norm_gain,
    soft_query,
    soft_key,
    soft_value,
    segment_of,
):
    place = lax.axis_index("seq").astype(jnp.int32)[None]
    shared = (lax.axis_index("head") * HEADS_DEV // Q_PER_KV).astype(jnp.int32)[None]
    head_shards = lax.axis_size("head")
    same_column = [[row * 8 + at for row in range(ROWS)] for at in range(8)]
    shifts = [
        [(at, at // 8 * 8 + (at + 2 * step) % 8) for at in range(SEGS)] for step in range(COLUMNS)
    ]
    partners = [(at, at ^ 1) for at in range(SEGS)]
    pieces = key_value_pieces(shared, soft_key, soft_value)
    column = lax.all_to_all(
        pieces, "seq", 0, 0, tiled=True, axis_index_groups=same_column
    )
    columns = [column] + [
        lax.ppermute(column, "seq", shifts[step]) for step in range(1, COLUMNS)
    ]
    local = local_memory(lin_key, lin_value, log_decay)
    received = lax.all_to_all(local, "seq", 0, 0, tiled=True)
    scanned = scan_memory(received)
    memory = lax.all_to_all(scanned, "seq", 0, 0, tiled=True)
    inside = inside_part(lin_query, lin_key, lin_value, log_decay)
    mixed, squares = mixed_part(lin_query, log_decay, inside, memory, head_shards)
    squares = lax.all_to_all(squares, "head", 0, 0, tiled=True)
    lin_out = gate_part(mixed, squares, norm_gain, out_gate)
    state = attend_own(segment_of, place, soft_query, pieces, column)
    *state, pairs = attend_shifted(segment_of, place, soft_query, columns, state)
    others = lax.ppermute(pairs, "seq", partners)
    soft_out = attend_swapped(segment_of, place, soft_query, others, state)
    return (lin_out, soft_out)


def solution(mesh):
    return jax.shard_map(
        shards,
        mesh=mesh,
        in_specs=(
            P("seq", "head"),
            P("seq", "head"),
            P("seq", "head"),
            P("head", "seq"),
            P("seq", "head"),
            P("head"),
            P("seq", "head"),
            P("seq", None),
            P("seq", None),
            P(),
        ),
        out_specs=(P("seq", "head"), P("seq", "head")),
        check_vma=False,
    )
```

```python
import jax
import jax.numpy as jnp
from jax import lax
from jax.experimental import pallas as pl
from jax.experimental.pallas import tpu as pltpu
from jax.sharding import PartitionSpec as P


HEAD_DIM = 128
HEADS_DEV = 4
Q_PER_KV = 8
TOK = 128
SEGS = 64
HALF = 32
ROWS = 8
COLUMNS = 4

norm_eps = 1e-06
SCALE = HEAD_DIM ** (-0.5)
LOG2E = 1.4426950408889634
F32 = jnp.float32
BF16 = jnp.bfloat16
MASKED = -1e30
VMEM_GRANT = 64 * 1024 * 1024

VM = pl.BlockSpec(memory_space=pltpu.VMEM)
SM = pl.BlockSpec(memory_space=pltpu.SMEM)


def dot(a, b, ca, cb, precision=None):
    return lax.dot_general(
        a, b, (((ca,), (cb,)), ((), ())), precision=precision, preferred_element_type=F32
    )


def iotas(n=TOK):
    return (
        lax.broadcasted_iota(jnp.int32, (n, TOK), 0),
        lax.broadcasted_iota(jnp.int32, (n, TOK), 1),
    )


def cumulative_columns(log_row):
    row, col = iotas()
    wide = jnp.broadcast_to(log_row, (TOK, TOK))
    column = jnp.sum(jnp.where(col <= row, wide, 0.0), axis=1, keepdims=True)
    log_column = jnp.sum(jnp.where(col == row, wide, 0.0), axis=1, keepdims=True)
    as_row = jnp.sum(jnp.where(row <= col, log_column, 0.0), axis=0, keepdims=True)
    return column, as_row


def split_bf16(value):
    high = value.astype(BF16)
    return high, (value - high.astype(F32)).astype(BF16)


def memory_kernel(key_ref, value_ref, log_ref, out_ref):
    for head in range(HEADS_DEV):
        lanes = slice(head * HEAD_DIM, (head + 1) * HEAD_DIM)
        column, _ = cumulative_columns(log_ref[head : head + 1, :])
        last = column[TOK - 1 :, :]
        weighted = key_ref[:, lanes].astype(F32) * jnp.exp(last - column)
        high, low = split_bf16(weighted)
        value = value_ref[:, lanes]
        local = dot(high, value, 0, 0) + dot(low, value, 0, 0)
        pieces = slice(head * 16, (head + 1) * 16)
        total = jnp.broadcast_to(last, (8, HEAD_DIM))
        first, _ = split_bf16(total)
        second, third = split_bf16(total - first.astype(F32))
        sub = lax.broadcasted_iota(jnp.int32, (8, HEAD_DIM), 0)
        parts = jnp.where(
            sub == 0,
            first.astype(F32),
            jnp.where(sub == 1, second.astype(F32), jnp.where(sub == 2, third.astype(F32), 0.0)),
        )
        both = jnp.concatenate(
            [local.reshape(16, 8, HEAD_DIM), jnp.broadcast_to(parts[None], (16, 8, HEAD_DIM))],
            axis=1,
        )
        out_ref[pieces] = both.astype(BF16)


def scan_kernel(in_ref, out_ref, wide_ref):
    wide_ref[...] = in_ref[...].astype(F32)
    block_log = wide_ref[:, 8, :] + wide_ref[:, 9, :] + wide_ref[:, 10, :]
    row, col = iotas(SEGS)
    later = jnp.where(row > col, block_log, 0.0)
    trow = lax.broadcasted_iota(jnp.int32, (SEGS, SEGS), 0)
    tcol = lax.broadcasted_iota(jnp.int32, (SEGS, SEGS), 1)
    before = jnp.where(tcol < trow, 1.0, 0.0)
    spread = dot(before, later, 1, 0, lax.Precision.HIGHEST)[:, :SEGS]
    decay = jnp.where(tcol < trow, jnp.exp(spread), 0.0)
    high, low = split_bf16(decay)
    for sub in range(8):
        data = wide_ref[:, sub, :].astype(BF16)
        wide_ref[:, sub, :] = dot(high, data, 1, 0) + dot(low, data, 1, 0)
    out_ref[...] = wide_ref[:, 0:8, :].astype(BF16)


def inside_kernel(query_ref, key_ref, value_ref, log_ref, out_ref):
    row, col = iotas()
    for head in range(HEADS_DEV):
        lanes = slice(head * HEAD_DIM, (head + 1) * HEAD_DIM)
        column, as_row = cumulative_columns(log_ref[head : head + 1, :])
        scores = dot(query_ref[:, lanes], key_ref[:, lanes], 1, 1)
        causal = col <= row
        decay = jnp.exp(jnp.where(causal, column - as_row, 0.0))
        mixing = jnp.where(causal, scores * decay, 0.0).astype(BF16)
        out_ref[:, lanes] = dot(mixing, value_ref[:, lanes], 1, 0)


def mixed_kernel(query_ref, log_ref, inside_ref, memory_ref, out_ref, square_ref):
    row, col = iotas()
    squares = jnp.zeros((TOK, HEAD_DIM), F32)
    for head in range(HEADS_DEV):
        lanes = slice(head * HEAD_DIM, (head + 1) * HEAD_DIM)
        column, _ = cumulative_columns(log_ref[head : head + 1, :])
        memory = memory_ref[head * 16 : (head + 1) * 16].astype(F32).reshape(HEAD_DIM, HEAD_DIM)
        earlier = dot(query_ref[:, lanes], memory.astype(BF16), 1, 0)
        mixed = inside_ref[:, lanes] + jnp.exp(column) * earlier
        out_ref[:, lanes] = mixed
        squares = squares + mixed * mixed
    total = jnp.sum(squares, axis=1, keepdims=True)
    total_row = jnp.sum(jnp.where(row == col, total, 0.0), axis=0, keepdims=True)
    square_ref[...] = jnp.broadcast_to(total_row[None], square_ref.shape)


def gate_kernel(mixed_ref, square_ref, gain_ref, gate_ref, out_ref):
    row, col = iotas()
    shards = square_ref.shape[0]
    total_row = square_ref[0, 0:1, :]
    for shard in range(1, shards):
        total_row = total_row + square_ref[shard, 0:1, :]
    total = jnp.sum(jnp.where(row == col, total_row, 0.0), axis=1, keepdims=True)
    inverse = lax.rsqrt(total / (HEADS_DEV * HEAD_DIM * shards) + norm_eps)
    gated = mixed_ref[...] * inverse * gain_ref[...] * jax.nn.sigmoid(gate_ref[...].astype(F32))
    out_ref[...] = gated.astype(BF16)


def pieces_kernel(place_ref, key_ref, value_ref, out_ref):
    out_ref[:, :, 0:HEAD_DIM] = jnp.broadcast_to(key_ref[...][None], (ROWS, TOK, HEAD_DIM))
    out_ref[:, :, HEAD_DIM:] = jnp.broadcast_to(value_ref[...][None], (ROWS, TOK, HEAD_DIM))


def stack_heads(query_ref, heads_ref):
    for head in range(HEADS_DEV):
        heads_ref[head * TOK : (head + 1) * TOK] = query_ref[:, head * HEAD_DIM : (head + 1) * HEAD_DIM]


def score_columns(pairs_ref, columns, core, place, seg_ref, heads_ref, score_ref, top_ref):
    own_segment = seg_ref[place]

    def score(column, carry):
        source = jnp.bitwise_and(place // 2 - column * (1 - 2 * core), COLUMNS - 1)
        keys = pairs_ref[pl.ds(column * ROWS, ROWS), :, 0:HEAD_DIM].reshape(ROWS * TOK, HEAD_DIM)
        logits = dot(heads_ref[...], keys, 1, 1)
        top = top_ref[...]
        for at in range(ROWS):
            seg = seg_ref[at * ROWS + source * 2 + core]
            part = logits[:, at * TOK : (at + 1) * TOK] + jnp.where(seg < own_segment, 0.0, MASKED).astype(F32)
            top = jnp.maximum(top, part)
            score_ref[column - columns[0], :, at * TOK : (at + 1) * TOK] = part
        top_ref[...] = top
        return carry

    lax.fori_loop(*columns, score, 0, unroll=2)


def weigh_columns(pairs_ref, columns, score_ref, peak_ref, total_ref, acc_ref):
    def weigh(column, carry):
        values = pairs_ref[pl.ds(column * ROWS, ROWS), :, HEAD_DIM:].reshape(ROWS * TOK, HEAD_DIM)
        peak = peak_ref[...]
        total = total_ref[...]
        low = []
        for at in range(ROWS):
            part = score_ref[column - columns[0], :, at * TOK : (at + 1) * TOK]
            weights = jnp.exp2((part - peak) * (SCALE * LOG2E))
            total = total + weights
            low.append(weights.astype(BF16))
        total_ref[...] = total
        acc_ref[...] += dot(jnp.concatenate(low, axis=1), values, 1, 0)
        return carry

    lax.fori_loop(*columns, weigh, 0)


def widest(top):
    return jnp.broadcast_to(jnp.max(top, axis=1, keepdims=True), top.shape)


def own_kernel(
    seg_ref, place_ref, query_ref, own_ref, column_ref,
    peak_ref, total_ref, acc_ref, heads_ref, score_ref, own_score_ref,
):
    place = place_ref[0]
    stack_heads(query_ref, heads_ref)
    row = jnp.bitwise_and(lax.broadcasted_iota(jnp.int32, (HEADS_DEV * TOK, TOK), 0), TOK - 1)
    col = lax.broadcasted_iota(jnp.int32, (HEADS_DEV * TOK, TOK), 1)
    logits = jnp.where(col <= row, dot(heads_ref[...], own_ref[0, :, 0:HEAD_DIM], 1, 1), MASKED)
    own_score_ref[...] = logits
    peak_ref[...] = logits
    score_columns(column_ref, (0, 1), place % 2, place, seg_ref, heads_ref, score_ref, peak_ref)
    peak_ref[...] = widest(peak_ref[...])
    weights = jnp.exp2((own_score_ref[...] - peak_ref[...]) * (SCALE * LOG2E))
    total_ref[...] = weights
    acc_ref[...] = dot(weights.astype(BF16), own_ref[0, :, HEAD_DIM:], 1, 0)
    weigh_columns(column_ref, (0, 1), score_ref, peak_ref, total_ref, acc_ref)


def later_columns(pairs_ref, columns, core, seg_ref, place, query_ref, old, new, scratch):
    heads_ref, score_ref = scratch
    old_peak_ref, old_total_ref, old_acc_ref = old
    peak_ref, total_ref, acc_ref = new
    stack_heads(query_ref, heads_ref)
    peak_ref[...] = old_peak_ref[...]
    score_columns(pairs_ref, columns, core, place, seg_ref, heads_ref, score_ref, peak_ref)
    peak = widest(peak_ref[...])
    peak_ref[...] = peak
    fade = jnp.exp2((old_peak_ref[...] - peak) * (SCALE * LOG2E))
    total_ref[...] = old_total_ref[...] * fade
    acc_ref[...] = old_acc_ref[...] * fade
    weigh_columns(pairs_ref, columns, score_ref, peak_ref, total_ref, acc_ref)


def shifted_kernel(
    seg_ref, place_ref, query_ref, zero_ref, one_ref, two_ref, three_ref,
    old_peak_ref, old_total_ref, old_acc_ref,
    peak_ref, total_ref, acc_ref, pairs_ref, heads_ref, score_ref,
):
    place = place_ref[0]
    for column, column_ref in enumerate((zero_ref, one_ref, two_ref, three_ref)):
        pairs_ref[column * ROWS : (column + 1) * ROWS] = column_ref[...]
    later_columns(
        pairs_ref, (1, COLUMNS), place % 2, seg_ref, place, query_ref,
        (old_peak_ref, old_total_ref, old_acc_ref), (peak_ref, total_ref, acc_ref),
        (heads_ref, score_ref),
    )


def swapped_kernel(
    seg_ref, place_ref, query_ref, pairs_ref,
    old_peak_ref, old_total_ref, old_acc_ref,
    out_ref, peak_ref, total_ref, acc_ref, heads_ref, score_ref,
):
    place = place_ref[0]
    later_columns(
        pairs_ref, (0, COLUMNS), 1 - place % 2, seg_ref, place, query_ref,
        (old_peak_ref, old_total_ref, old_acc_ref), (peak_ref, total_ref, acc_ref),
        (heads_ref, score_ref),
    )
    for head in range(HEADS_DEV):
        rows = slice(head * TOK, (head + 1) * TOK)
        total = jnp.sum(total_ref[rows], axis=1, keepdims=True)
        out_ref[:, head * HEAD_DIM : (head + 1) * HEAD_DIM] = (acc_ref[rows] / total).astype(BF16)


def shape(*dims, dtype=F32):
    return jax.ShapeDtypeStruct(dims, dtype)


def local_memory(key, value, log_decay):
    return pl.pallas_call(
        memory_kernel, name="memory", compiler_params=pltpu.CompilerParams(vmem_limit_bytes=VMEM_GRANT), out_shape=shape(SEGS, 16, HEAD_DIM, dtype=BF16),
        in_specs=[VM] * 3, out_specs=VM,
    )(key, value, log_decay)


def scan_memory(received):
    return pl.pallas_call(
        scan_kernel, name="scan", compiler_params=pltpu.CompilerParams(vmem_limit_bytes=VMEM_GRANT), out_shape=shape(SEGS, 8, HEAD_DIM, dtype=BF16),
        in_specs=[VM], out_specs=VM, scratch_shapes=[pltpu.VMEM((SEGS, 16, HEAD_DIM), F32)],
    )(received)


def inside_part(query, key, value, log_decay):
    return pl.pallas_call(
        inside_kernel, name="inside", compiler_params=pltpu.CompilerParams(vmem_limit_bytes=VMEM_GRANT), out_shape=shape(TOK, HEADS_DEV * HEAD_DIM),
        in_specs=[VM] * 4, out_specs=VM,
    )(query, key, value, log_decay)


def mixed_part(query, log_decay, inside, memory, shards):
    return pl.pallas_call(
        mixed_kernel, name="mixed", compiler_params=pltpu.CompilerParams(vmem_limit_bytes=VMEM_GRANT),
        out_shape=(shape(TOK, HEADS_DEV * HEAD_DIM), shape(shards, 8, TOK)),
        in_specs=[VM] * 4, out_specs=(VM, VM),
    )(query, log_decay, inside, memory)


def gate_part(mixed, squares, gain, gate):
    return pl.pallas_call(
        gate_kernel, name="gate", compiler_params=pltpu.CompilerParams(vmem_limit_bytes=VMEM_GRANT), out_shape=shape(TOK, HEADS_DEV * HEAD_DIM, dtype=BF16),
        in_specs=[VM] * 4, out_specs=VM,
    )(mixed, squares, gain[None, :], gate)


def key_value_pieces(place, key, value):
    return pl.pallas_call(
        pieces_kernel, name="pieces", compiler_params=pltpu.CompilerParams(vmem_limit_bytes=VMEM_GRANT),
        out_shape=shape(ROWS, TOK, 2 * HEAD_DIM, dtype=BF16),
        grid_spec=pltpu.PrefetchScalarGridSpec(
            num_scalar_prefetch=1,
            grid=(1,),
            in_specs=[
                pl.BlockSpec((TOK, HEAD_DIM), lambda i, at: (0, at[0])),
                pl.BlockSpec((TOK, HEAD_DIM), lambda i, at: (0, at[0])),
            ],
            out_specs=pl.BlockSpec((ROWS, TOK, 2 * HEAD_DIM), lambda i, at: (0, 0, 0)),
        ),
    )(place, key, value)


STACKED = HEADS_DEV * TOK


def state_scratch(count):
    return [pltpu.VMEM((STACKED, HEAD_DIM), F32)] * count


def score_scratch(columns):
    return [
        pltpu.VMEM((STACKED, HEAD_DIM), BF16),
        pltpu.VMEM((columns, STACKED, ROWS * TOK), F32),
    ]


def attend_own(segment_of, place, query, pieces, column):
    whole = lambda *dims: pl.BlockSpec(dims, lambda i: (0,) * len(dims))
    return pl.pallas_call(
        own_kernel, name="own", compiler_params=pltpu.CompilerParams(vmem_limit_bytes=VMEM_GRANT),
        out_shape=(shape(STACKED, HEAD_DIM),) * 3,
        grid=(1,),
        in_specs=[
            SM, SM, whole(TOK, HEADS_DEV * HEAD_DIM), whole(1, TOK, 2 * HEAD_DIM),
            whole(ROWS, TOK, 2 * HEAD_DIM),
        ],
        out_specs=(whole(STACKED, HEAD_DIM),) * 3,
        scratch_shapes=score_scratch(1) + state_scratch(1),
    )(segment_of, place, query, pieces, column)


def attend_shifted(segment_of, place, query, columns, state):
    return pl.pallas_call(
        shifted_kernel, name="shifted", compiler_params=pltpu.CompilerParams(vmem_limit_bytes=VMEM_GRANT),
        out_shape=(shape(STACKED, HEAD_DIM),) * 3 + (shape(HALF, TOK, 2 * HEAD_DIM, dtype=BF16),),
        in_specs=[SM, SM] + [VM] * 8, out_specs=(VM,) * 4,
        scratch_shapes=score_scratch(COLUMNS - 1),
    )(segment_of, place, query, *columns, *state)


def attend_swapped(segment_of, place, query, pairs, state):
    return pl.pallas_call(
        swapped_kernel, name="swapped", compiler_params=pltpu.CompilerParams(vmem_limit_bytes=VMEM_GRANT),
        out_shape=shape(TOK, HEADS_DEV * HEAD_DIM, dtype=BF16),
        in_specs=[SM, SM] + [VM] * 5, out_specs=VM,
        scratch_shapes=state_scratch(3) + score_scratch(COLUMNS),
    )(segment_of, place, query, pairs, *state)


def shards(
    lin_query,
    lin_key,
    lin_value,
    log_decay,
    out_gate,
    norm_gain,
    soft_query,
    soft_key,
    soft_value,
    segment_of,
):
    place = lax.axis_index("seq").astype(jnp.int32)[None]
    shared = lax.div(lax.axis_index("head").astype(jnp.int32), Q_PER_KV // HEADS_DEV)[None]
    head_shards = lax.axis_size("head")
    same_column = [[row * 8 + at for row in range(ROWS)] for at in range(8)]
    ahead = [(at, at // 8 * 8 + (at + 2 * (1 - 2 * (at % 2))) % 8) for at in range(SEGS)]
    back = [(there, here) for here, there in ahead]
    partners = [(at, at ^ 1) for at in range(SEGS)]
    pieces = key_value_pieces(shared, soft_key, soft_value)
    column = lax.all_to_all(
        pieces, "seq", 0, 0, tiled=True, axis_index_groups=same_column
    )
    nearest = lax.ppermute(column, "seq", ahead)
    behind = lax.ppermute(column, "seq", back)
    farthest = lax.ppermute(nearest, "seq", ahead)
    columns = [column, nearest, farthest, behind]
    local = local_memory(lin_key, lin_value, log_decay)
    received = lax.all_to_all(local, "seq", 0, 0, tiled=True)
    scanned = scan_memory(received)
    memory = lax.all_to_all(scanned, "seq", 0, 0, tiled=True)
    inside = inside_part(lin_query, lin_key, lin_value, log_decay)
    mixed, squares = mixed_part(lin_query, log_decay, inside, memory, head_shards)
    squares = lax.all_to_all(squares, "head", 0, 0, tiled=True)
    lin_out = gate_part(mixed, squares, norm_gain, out_gate)
    state = attend_own(segment_of, place, soft_query, pieces, column)
    *state, pairs = attend_shifted(segment_of, place, soft_query, columns, state)
    others = lax.ppermute(pairs, "seq", partners)
    soft_out = attend_swapped(segment_of, place, soft_query, others, state)
    return (lin_out, soft_out)


def solution(mesh):
    return jax.shard_map(
        shards,
        mesh=mesh,
        in_specs=(
            P("seq", "head"),
            P("seq", "head"),
            P("seq", "head"),
            P("head", "seq"),
            P("seq", "head"),
            P("head"),
            P("seq", "head"),
            P("seq", None),
            P("seq", None),
            P(),
        ),
        out_specs=(P("seq", "head"), P("seq", "head")),
        check_vma=False,
    )
```

```python
import jax
import jax.numpy as jnp
from jax import lax
from jax.experimental import pallas as pl
from jax.experimental.pallas import tpu as pltpu
from jax.sharding import PartitionSpec as P


HEAD_DIM = 128
HEADS_DEV = 4
Q_PER_KV = 8
TOK = 128
SEGS = 64
HALF = 32
ROWS = 8
COLUMNS = 4
TURN = 4

norm_eps = 1e-06
SCALE = HEAD_DIM ** (-0.5)
LOG2E = 1.4426950408889634
F32 = jnp.float32
BF16 = jnp.bfloat16
MASKED = -1e30
VMEM_GRANT = 64 * 1024 * 1024

VM = pl.BlockSpec(memory_space=pltpu.VMEM)
SM = pl.BlockSpec(memory_space=pltpu.SMEM)


def dot(a, b, ca, cb, precision=None):
    return lax.dot_general(
        a, b, (((ca,), (cb,)), ((), ())), precision=precision, preferred_element_type=F32
    )


def iotas(n=TOK):
    return (
        lax.broadcasted_iota(jnp.int32, (n, TOK), 0),
        lax.broadcasted_iota(jnp.int32, (n, TOK), 1),
    )


def cumulative_columns(log_row):
    row, col = iotas()
    wide = jnp.broadcast_to(log_row, (TOK, TOK))
    column = jnp.sum(jnp.where(col <= row, wide, 0.0), axis=1, keepdims=True)
    log_column = jnp.sum(jnp.where(col == row, wide, 0.0), axis=1, keepdims=True)
    as_row = jnp.sum(jnp.where(row <= col, log_column, 0.0), axis=0, keepdims=True)
    return column, as_row


def split_bf16(value):
    high = value.astype(BF16)
    return high, (value - high.astype(F32)).astype(BF16)


def memory_kernel(key_ref, value_ref, log_ref, out_ref):
    for head in range(HEADS_DEV):
        lanes = slice(head * HEAD_DIM, (head + 1) * HEAD_DIM)
        column, _ = cumulative_columns(log_ref[head : head + 1, :])
        last = column[TOK - 1 :, :]
        weighted = key_ref[:, lanes].astype(F32) * jnp.exp(last - column)
        high, low = split_bf16(weighted)
        value = value_ref[:, lanes]
        local = dot(high, value, 0, 0) + dot(low, value, 0, 0)
        pieces = slice(head * 16, (head + 1) * 16)
        total = jnp.broadcast_to(last, (8, HEAD_DIM))
        first, _ = split_bf16(total)
        second, third = split_bf16(total - first.astype(F32))
        sub = lax.broadcasted_iota(jnp.int32, (8, HEAD_DIM), 0)
        parts = jnp.where(
            sub == 0,
            first.astype(F32),
            jnp.where(sub == 1, second.astype(F32), jnp.where(sub == 2, third.astype(F32), 0.0)),
        )
        both = jnp.concatenate(
            [local.reshape(16, 8, HEAD_DIM), jnp.broadcast_to(parts[None], (16, 8, HEAD_DIM))],
            axis=1,
        )
        out_ref[pieces] = both.astype(BF16)


def scan_kernel(in_ref, out_ref, wide_ref):
    wide_ref[...] = in_ref[...].astype(F32)
    block_log = wide_ref[:, 8, :] + wide_ref[:, 9, :] + wide_ref[:, 10, :]
    row, col = iotas(SEGS)
    later = jnp.where(row > col, block_log, 0.0)
    trow = lax.broadcasted_iota(jnp.int32, (SEGS, SEGS), 0)
    tcol = lax.broadcasted_iota(jnp.int32, (SEGS, SEGS), 1)
    before = jnp.where(tcol < trow, 1.0, 0.0)
    spread = dot(before, later, 1, 0, lax.Precision.HIGHEST)[:, :SEGS]
    decay = jnp.where(tcol < trow, jnp.exp(spread), 0.0)
    high, low = split_bf16(decay)
    for sub in range(8):
        data = wide_ref[:, sub, :].astype(BF16)
        wide_ref[:, sub, :] = dot(high, data, 1, 0) + dot(low, data, 1, 0)
    out_ref[...] = wide_ref[:, 0:8, :].astype(BF16)


def inside_kernel(query_ref, key_ref, value_ref, log_ref, out_ref):
    row, col = iotas()
    for head in range(HEADS_DEV):
        lanes = slice(head * HEAD_DIM, (head + 1) * HEAD_DIM)
        column, as_row = cumulative_columns(log_ref[head : head + 1, :])
        scores = dot(query_ref[:, lanes], key_ref[:, lanes], 1, 1)
        causal = col <= row
        decay = jnp.exp(jnp.where(causal, column - as_row, 0.0))
        mixing = jnp.where(causal, scores * decay, 0.0).astype(BF16)
        out_ref[:, lanes] = dot(mixing, value_ref[:, lanes], 1, 0)


def mixed_kernel(query_ref, log_ref, inside_ref, memory_ref, out_ref, square_ref):
    row, col = iotas()
    squares = jnp.zeros((TOK, HEAD_DIM), F32)
    for head in range(HEADS_DEV):
        lanes = slice(head * HEAD_DIM, (head + 1) * HEAD_DIM)
        column, _ = cumulative_columns(log_ref[head : head + 1, :])
        memory = memory_ref[head * 16 : (head + 1) * 16].astype(F32).reshape(HEAD_DIM, HEAD_DIM)
        earlier = dot(query_ref[:, lanes], memory.astype(BF16), 1, 0)
        mixed = inside_ref[:, lanes] + jnp.exp(column) * earlier
        out_ref[:, lanes] = mixed
        squares = squares + mixed * mixed
    total = jnp.sum(squares, axis=1, keepdims=True)
    total_row = jnp.sum(jnp.where(row == col, total, 0.0), axis=0, keepdims=True)
    square_ref[...] = jnp.broadcast_to(total_row[None], square_ref.shape)


def gate_kernel(mixed_ref, square_ref, gain_ref, gate_ref, out_ref):
    row, col = iotas()
    shards = square_ref.shape[0]
    total_row = square_ref[0, 0:1, :]
    for shard in range(1, shards):
        total_row = total_row + square_ref[shard, 0:1, :]
    total = jnp.sum(jnp.where(row == col, total_row, 0.0), axis=1, keepdims=True)
    inverse = lax.rsqrt(total / (HEADS_DEV * HEAD_DIM * shards) + norm_eps)
    gated = mixed_ref[...] * inverse * gain_ref[...] * jax.nn.sigmoid(gate_ref[...].astype(F32))
    out_ref[...] = gated.astype(BF16)


def pieces_kernel(place_ref, key_ref, value_ref, out_ref):
    out_ref[:, :, 0:HEAD_DIM] = jnp.broadcast_to(key_ref[...][None], (ROWS, TOK, HEAD_DIM))
    out_ref[:, :, HEAD_DIM:] = jnp.broadcast_to(value_ref[...][None], (ROWS, TOK, HEAD_DIM))


def stack_heads(query_ref, heads_ref):
    for head in range(HEADS_DEV):
        heads_ref[head * TOK : (head + 1) * TOK] = query_ref[:, head * HEAD_DIM : (head + 1) * HEAD_DIM]


def score_columns(pairs_ref, columns, core, place, seg_ref, heads_ref, score_ref, top_ref):
    own_segment = seg_ref[place]

    def score(column, carry):
        source = jnp.bitwise_and(place // 2 - column * (1 - 2 * core), COLUMNS - 1)
        keys = pairs_ref[pl.ds(column * ROWS, ROWS), :, 0:HEAD_DIM].reshape(ROWS * TOK, HEAD_DIM)
        logits = dot(heads_ref[...], keys, 1, 1)
        top = top_ref[...]
        for at in range(ROWS):
            row = jnp.bitwise_and(at + TURN * core, ROWS - 1)
            seg = seg_ref[row * ROWS + source * 2 + core]
            part = logits[:, at * TOK : (at + 1) * TOK] + jnp.where(seg < own_segment, 0.0, MASKED).astype(F32)
            top = jnp.maximum(top, part)
            score_ref[column - columns[0], :, at * TOK : (at + 1) * TOK] = part
        top_ref[...] = top
        return carry

    lax.fori_loop(*columns, score, 0, unroll=2)


def weigh_columns(pairs_ref, columns, score_ref, peak_ref, total_ref, acc_ref):
    def weigh(column, carry):
        values = pairs_ref[pl.ds(column * ROWS, ROWS), :, HEAD_DIM:].reshape(ROWS * TOK, HEAD_DIM)
        peak = peak_ref[...]
        total = total_ref[...]
        low = []
        for at in range(ROWS):
            part = score_ref[column - columns[0], :, at * TOK : (at + 1) * TOK]
            weights = jnp.exp2((part - peak) * (SCALE * LOG2E))
            total = total + weights
            low.append(weights.astype(BF16))
        total_ref[...] = total
        acc_ref[...] += dot(jnp.concatenate(low, axis=1), values, 1, 0)
        return carry

    lax.fori_loop(*columns, weigh, 0)


def widest(top):
    return jnp.broadcast_to(jnp.max(top, axis=1, keepdims=True), top.shape)


def own_kernel(
    seg_ref, place_ref, query_ref, own_ref, column_ref,
    peak_ref, total_ref, acc_ref, heads_ref, score_ref, own_score_ref,
):
    place = place_ref[0]
    stack_heads(query_ref, heads_ref)
    row = jnp.bitwise_and(lax.broadcasted_iota(jnp.int32, (HEADS_DEV * TOK, TOK), 0), TOK - 1)
    col = lax.broadcasted_iota(jnp.int32, (HEADS_DEV * TOK, TOK), 1)
    logits = jnp.where(col <= row, dot(heads_ref[...], own_ref[0, :, 0:HEAD_DIM], 1, 1), MASKED)
    own_score_ref[...] = logits
    peak_ref[...] = logits
    score_columns(column_ref, (0, 1), place % 2, place, seg_ref, heads_ref, score_ref, peak_ref)
    peak_ref[...] = widest(peak_ref[...])
    weights = jnp.exp2((own_score_ref[...] - peak_ref[...]) * (SCALE * LOG2E))
    total_ref[...] = weights
    acc_ref[...] = dot(weights.astype(BF16), own_ref[0, :, HEAD_DIM:], 1, 0)
    weigh_columns(column_ref, (0, 1), score_ref, peak_ref, total_ref, acc_ref)


def later_columns(pairs_ref, columns, core, seg_ref, place, query_ref, old, new, scratch):
    heads_ref, score_ref = scratch
    old_peak_ref, old_total_ref, old_acc_ref = old
    peak_ref, total_ref, acc_ref = new
    stack_heads(query_ref, heads_ref)
    peak_ref[...] = old_peak_ref[...]
    score_columns(pairs_ref, columns, core, place, seg_ref, heads_ref, score_ref, peak_ref)
    peak = widest(peak_ref[...])
    peak_ref[...] = peak
    fade = jnp.exp2((old_peak_ref[...] - peak) * (SCALE * LOG2E))
    total_ref[...] = old_total_ref[...] * fade
    acc_ref[...] = old_acc_ref[...] * fade
    weigh_columns(pairs_ref, columns, score_ref, peak_ref, total_ref, acc_ref)


def shifted_kernel(
    seg_ref, place_ref, query_ref, zero_ref, one_ref, two_ref, three_ref,
    old_peak_ref, old_total_ref, old_acc_ref,
    peak_ref, total_ref, acc_ref, pairs_ref, heads_ref, score_ref,
):
    place = place_ref[0]
    for column, column_ref in enumerate((zero_ref, one_ref, two_ref, three_ref)):
        pairs_ref[column * ROWS : (column + 1) * ROWS] = column_ref[...]
    later_columns(
        pairs_ref, (1, COLUMNS), place % 2, seg_ref, place, query_ref,
        (old_peak_ref, old_total_ref, old_acc_ref), (peak_ref, total_ref, acc_ref),
        (heads_ref, score_ref),
    )


def swapped_kernel(
    seg_ref, place_ref, query_ref, pairs_ref,
    old_peak_ref, old_total_ref, old_acc_ref,
    out_ref, peak_ref, total_ref, acc_ref, heads_ref, score_ref,
):
    place = place_ref[0]
    later_columns(
        pairs_ref, (0, COLUMNS), 1 - place % 2, seg_ref, place, query_ref,
        (old_peak_ref, old_total_ref, old_acc_ref), (peak_ref, total_ref, acc_ref),
        (heads_ref, score_ref),
    )
    for head in range(HEADS_DEV):
        rows = slice(head * TOK, (head + 1) * TOK)
        total = jnp.sum(total_ref[rows], axis=1, keepdims=True)
        out_ref[:, head * HEAD_DIM : (head + 1) * HEAD_DIM] = (acc_ref[rows] / total).astype(BF16)


def shape(*dims, dtype=F32):
    return jax.ShapeDtypeStruct(dims, dtype)


def local_memory(key, value, log_decay):
    return pl.pallas_call(
        memory_kernel, name="memory", compiler_params=pltpu.CompilerParams(vmem_limit_bytes=VMEM_GRANT), out_shape=shape(SEGS, 16, HEAD_DIM, dtype=BF16),
        in_specs=[VM] * 3, out_specs=VM,
    )(key, value, log_decay)


def scan_memory(received):
    return pl.pallas_call(
        scan_kernel, name="scan", compiler_params=pltpu.CompilerParams(vmem_limit_bytes=VMEM_GRANT), out_shape=shape(SEGS, 8, HEAD_DIM, dtype=BF16),
        in_specs=[VM], out_specs=VM, scratch_shapes=[pltpu.VMEM((SEGS, 16, HEAD_DIM), F32)],
    )(received)


def inside_part(query, key, value, log_decay):
    return pl.pallas_call(
        inside_kernel, name="inside", compiler_params=pltpu.CompilerParams(vmem_limit_bytes=VMEM_GRANT), out_shape=shape(TOK, HEADS_DEV * HEAD_DIM),
        in_specs=[VM] * 4, out_specs=VM,
    )(query, key, value, log_decay)


def mixed_part(query, log_decay, inside, memory, shards):
    return pl.pallas_call(
        mixed_kernel, name="mixed", compiler_params=pltpu.CompilerParams(vmem_limit_bytes=VMEM_GRANT),
        out_shape=(shape(TOK, HEADS_DEV * HEAD_DIM), shape(shards, 8, TOK)),
        in_specs=[VM] * 4, out_specs=(VM, VM),
    )(query, log_decay, inside, memory)


def gate_part(mixed, squares, gain, gate):
    return pl.pallas_call(
        gate_kernel, name="gate", compiler_params=pltpu.CompilerParams(vmem_limit_bytes=VMEM_GRANT), out_shape=shape(TOK, HEADS_DEV * HEAD_DIM, dtype=BF16),
        in_specs=[VM] * 4, out_specs=VM,
    )(mixed, squares, gain[None, :], gate)


def key_value_pieces(place, key, value):
    return pl.pallas_call(
        pieces_kernel, name="pieces", compiler_params=pltpu.CompilerParams(vmem_limit_bytes=VMEM_GRANT),
        out_shape=shape(ROWS, TOK, 2 * HEAD_DIM, dtype=BF16),
        grid_spec=pltpu.PrefetchScalarGridSpec(
            num_scalar_prefetch=1,
            grid=(1,),
            in_specs=[
                pl.BlockSpec((TOK, HEAD_DIM), lambda i, at: (0, at[0])),
                pl.BlockSpec((TOK, HEAD_DIM), lambda i, at: (0, at[0])),
            ],
            out_specs=pl.BlockSpec((ROWS, TOK, 2 * HEAD_DIM), lambda i, at: (0, 0, 0)),
        ),
    )(place, key, value)


STACKED = HEADS_DEV * TOK


def state_scratch(count):
    return [pltpu.VMEM((STACKED, HEAD_DIM), F32)] * count


def score_scratch(columns):
    return [
        pltpu.VMEM((STACKED, HEAD_DIM), BF16),
        pltpu.VMEM((columns, STACKED, ROWS * TOK), F32),
    ]


def attend_own(segment_of, place, query, pieces, column):
    whole = lambda *dims: pl.BlockSpec(dims, lambda i: (0,) * len(dims))
    return pl.pallas_call(
        own_kernel, name="own", compiler_params=pltpu.CompilerParams(vmem_limit_bytes=VMEM_GRANT),
        out_shape=(shape(STACKED, HEAD_DIM),) * 3,
        grid=(1,),
        in_specs=[
            SM, SM, whole(TOK, HEADS_DEV * HEAD_DIM), whole(1, TOK, 2 * HEAD_DIM),
            whole(ROWS, TOK, 2 * HEAD_DIM),
        ],
        out_specs=(whole(STACKED, HEAD_DIM),) * 3,
        scratch_shapes=score_scratch(1) + state_scratch(1),
    )(segment_of, place, query, pieces, column)


def attend_shifted(segment_of, place, query, columns, state):
    return pl.pallas_call(
        shifted_kernel, name="shifted", compiler_params=pltpu.CompilerParams(vmem_limit_bytes=VMEM_GRANT),
        out_shape=(shape(STACKED, HEAD_DIM),) * 3 + (shape(HALF, TOK, 2 * HEAD_DIM, dtype=BF16),),
        in_specs=[SM, SM] + [VM] * 8, out_specs=(VM,) * 4,
        scratch_shapes=score_scratch(COLUMNS - 1),
    )(segment_of, place, query, *columns, *state)


def attend_swapped(segment_of, place, query, pairs, state):
    return pl.pallas_call(
        swapped_kernel, name="swapped", compiler_params=pltpu.CompilerParams(vmem_limit_bytes=VMEM_GRANT),
        out_shape=shape(TOK, HEADS_DEV * HEAD_DIM, dtype=BF16),
        in_specs=[SM, SM] + [VM] * 5, out_specs=VM,
        scratch_shapes=state_scratch(3) + score_scratch(COLUMNS),
    )(segment_of, place, query, pairs, *state)


def shards(
    lin_query,
    lin_key,
    lin_value,
    log_decay,
    out_gate,
    norm_gain,
    soft_query,
    soft_key,
    soft_value,
    segment_of,
):
    place = lax.axis_index("seq").astype(jnp.int32)[None]
    shared = lax.div(lax.axis_index("head").astype(jnp.int32), Q_PER_KV // HEADS_DEV)[None]
    head_shards = lax.axis_size("head")
    same_column = [
        [(rank + TURN * (at % 2)) % ROWS * 8 + at for rank in range(ROWS)] for at in range(8)
    ]
    ahead = [(at, at // 8 * 8 + (at + 2 * (1 - 2 * (at % 2))) % 8) for at in range(SEGS)]
    back = [(there, here) for here, there in ahead]
    partners = [(at, at ^ 1) for at in range(SEGS)]
    pieces = key_value_pieces(shared, soft_key, soft_value)
    column = lax.all_to_all(
        pieces, "seq", 0, 0, tiled=True, axis_index_groups=same_column
    )
    nearest = lax.ppermute(column, "seq", ahead)
    behind = lax.ppermute(column, "seq", back)
    farthest = lax.ppermute(nearest, "seq", ahead)
    columns = [column, nearest, farthest, behind]
    local = local_memory(lin_key, lin_value, log_decay)
    received = lax.all_to_all(local, "seq", 0, 0, tiled=True)
    scanned = scan_memory(received)
    memory = lax.all_to_all(scanned, "seq", 0, 0, tiled=True)
    inside = inside_part(lin_query, lin_key, lin_value, log_decay)
    mixed, squares = mixed_part(lin_query, log_decay, inside, memory, head_shards)
    squares = lax.all_to_all(squares, "head", 0, 0, tiled=True)
    lin_out = gate_part(mixed, squares, norm_gain, out_gate)
    state = attend_own(segment_of, place, soft_query, pieces, column)
    *state, pairs = attend_shifted(segment_of, place, soft_query, columns, state)
    others = lax.ppermute(pairs, "seq", partners)
    soft_out = attend_swapped(segment_of, place, soft_query, others, state)
    return (lin_out, soft_out)


def solution(mesh):
    return jax.shard_map(
        shards,
        mesh=mesh,
        in_specs=(
            P("seq", "head"),
            P("seq", "head"),
            P("seq", "head"),
            P("head", "seq"),
            P("seq", "head"),
            P("head"),
            P("seq", "head"),
            P("seq", None),
            P("seq", None),
            P(),
        ),
        out_specs=(P("seq", "head"), P("seq", "head")),
        check_vma=False,
    )
```
